256 devices in a mesh: tm: 128 (over x, z_lo, y, core), mp: 2 (over z_hi).
Axes of the slice: x: 4, y: 4, z: 8 (z_hi: 2, z_lo: 4; z = z_hi * 4 + z_lo), core: 2. Of those that a mesh axis runs over, the one named last changes fastest.
Arguments:
- filterbank: bfloat16 [4, 131072, 80], P(None, 'tm'), may hold values from -6 to 6
- lengths: int32 [4], replicated, may hold values from 16384 to 32768, as said below
- bank_begin: int32 [4, 8192], P(None, 'tm'), may hold values from 0 to 8191, as said below
- memory_in: bfloat16 [4, 8192, 1024], P(None, 'tm', 'mp'), may hold values from -6 to 6
- w_front: bfloat16 [320, 1024], P(None, 'mp'), may hold values from -0.3125 to 0.3125
- gain_attn: float32 [1024], replicated, may hold values from 0.25 to 1.75
- w_query: bfloat16 [1024, 1024], P(None, 'mp'), may hold values from -0.1875 to 0.1875
- w_key: bfloat16 [1024, 1024], P(None, 'mp'), may hold values from -0.1875 to 0.1875
- w_value: bfloat16 [1024, 1024], P(None, 'mp'), may hold values from -0.1875 to 0.1875
- w_out: bfloat16 [1024, 1024], P('mp'), may hold values from -0.1875 to 0.1875
- gain_ffn: float32 [1024], replicated, may hold values from 0.25 to 1.75
- w_up: bfloat16 [1024, 4096], P(None, 'mp'), may hold values from -0.1875 to 0.1875
- w_down: bfloat16 [4096, 1024], P('mp'), may hold values from -0.09375 to 0.09375
Outputs:
- encoded: bfloat16 [4, 32768, 1024], P(None, 'tm', 'mp')
- memory_out: bfloat16 [4, 8192, 1024], P(None, 'tm', 'mp')
The draws below stay inside these ranges and needn't reach their ends.
Inputs may be any that keep to these rules, and one draw needn't show every extreme that they name: `lengths`: some utterance has all 32768 frames. For segment i: max(0, i - 32) <= bank_begin <= max(0, i - 16); in each utterance some segment has bank_begin = i - 32.
All inputs are finite; a program needn't handle non-finite values.
Results may differ from the reference program's by a relative error of at most 0.012.
Values may be sent and summed in bfloat16 or wider, within the bound.
No kernel may reach another device: no remote copies, remote signals or barrier semaphores. Data moves between devices by JAX's collectives and lax.ppermute only.
A program may use at most 128 MiB of HBM per device.

```python
import jax
import jax.numpy as jnp
from jax import lax

D = 1024
HEAD_DIM = 64
FF = 4096
FBANK = 80
STACK = 4
SEG = 4
LC = 32
RC = 4
M = 32
UTT = 4
FRAMES = 32768
SEGMENTS = 8192
N_MP = 2


def draw_lengths(key, part):
    lower_end = FRAMES // 2
    drawn = jax.random.randint(jax.random.fold_in(key, 11), (UTT,), lower_end, FRAMES + 1)
    full_one = jax.random.randint(jax.random.fold_in(key, 12), (), 0, UTT)
    return jnp.where(jnp.arange(UTT) == full_one, FRAMES, drawn).astype(jnp.int32)


def draw_bank_begin(key, part):
    bank_span = jax.random.randint(jax.random.fold_in(key, 21), (UTT, SEGMENTS), M // 2, M + 1)
    chosen = jax.random.randint(jax.random.fold_in(key, 22), (UTT,), M, SEGMENTS)
    seg_index = jnp.arange(SEGMENTS, dtype=jnp.int32)
    bank_span = jnp.where(seg_index[None, :] == chosen[:, None], M, bank_span)
    return jnp.maximum(seg_index[None, :] - bank_span, 0).astype(jnp.int32)


def block_levels(rng, shape, cuts, smallest, top_value):
    def one(axis_at, shards_of):
        draws = jax.random.uniform(jax.random.fold_in(jax.random.fold_in(rng, 6), axis_at), (shards_of,), jnp.float32, smallest / len(cuts), top_value / len(cuts))
        return jnp.repeat(jnp.exp(draws), shape[axis_at] // shards_of).reshape((-1,) + (1,) * (len(shape) - axis_at - 1))

    level = one(*cuts[0])
    for cut in cuts[1:]:
        level = level * one(*cut)
    return level


def centred(rng, extent, scale, bound, split=(), held_as=jnp.bfloat16):
    values = scale * jax.random.normal(rng, extent, jnp.float32)
    if split:
        values = values * block_levels(rng, extent, split, -0.22, 0.18)
    return jnp.clip(values, -bound, bound).astype(held_as)


def setup_inputs(seed: int = 0) -> dict:
    key_of = jax.random.split(jax.random.key(seed), 14)
    filterbank = centred(key_of[0], (UTT, STACK * FRAMES, FBANK), 1.0, 6.0, ((1, 128),))
    lengths = draw_lengths(jax.random.fold_in(key_of[13], 71), 0)
    bank_begin = draw_bank_begin(jax.random.fold_in(key_of[13], 71), 0)
    memory_in = centred(key_of[3], (UTT, SEGMENTS, D), 1.0, 6.0, ((1, 128), (2, 2)))
    w_front = centred(key_of[4], (STACK * FBANK, D), (STACK * FBANK) ** -0.5, 0.3125, ((1, 2),))
    gain_attn = jnp.clip(1.0 + 0.15 * jax.random.normal(key_of[5], (D,), jnp.float32), 0.25, 1.75)
    w_query = centred(key_of[6], (D, D), D ** -0.5, 0.1875, ((1, 2),))
    w_key = centred(key_of[7], (D, D), D ** -0.5, 0.1875, ((1, 2),))
    w_value = centred(key_of[8], (D, D), D ** -0.5, 0.1875, ((1, 2),))
    w_out = centred(key_of[9], (D, D), D ** -0.5, 0.1875, ((0, 2),))
    gain_ffn = jnp.clip(1.0 + 0.15 * jax.random.normal(key_of[10], (D,), jnp.float32), 0.25, 1.75)
    w_up = centred(key_of[11], (D, FF), D ** -0.5, 0.1875, ((1, 2),))
    w_down = centred(key_of[12], (FF, D), FF ** -0.5, 0.09375, ((0, 2),))
    return {"filterbank": filterbank, "lengths": lengths, "bank_begin": bank_begin, "memory_in": memory_in, "w_front": w_front, "gain_attn": gain_attn, "w_query": w_query, "w_key": w_key, "w_value": w_value, "w_out": w_out, "gain_ffn": gain_ffn, "w_up": w_up, "w_down": w_down}


epsilon = 1e-05

def normalize(values, gain):
    center = lax.optimization_barrier(jnp.mean(values, axis=-1, keepdims=True))
    shifted = values - center
    spread = lax.optimization_barrier(jnp.mean(shifted * shifted, axis=-1, keepdims=True))
    return shifted * lax.rsqrt(spread + epsilon) * gain.astype(jnp.float32)

def product(inputs, weight):
    flat_rows = inputs.reshape(-1, inputs.shape[-1])
    result = jnp.dot(flat_rows, weight, preferred_element_type=jnp.float32)
    return result.reshape(inputs.shape[:-1] + (weight.shape[1],))

def grouped_product(inputs, weight):
    group_width = inputs.shape[-1] // N_MP
    running = jnp.zeros(inputs.shape[:-1] + (weight.shape[1],), jnp.float32)
    for group_index in range(N_MP):
        input_part = inputs[..., group_index * group_width:(group_index + 1) * group_width]
        weight_part = weight[group_index * group_width:(group_index + 1) * group_width]
        term_value = lax.optimization_barrier(product(input_part, weight_part).astype(jnp.bfloat16))
        running = running + term_value.astype(jnp.float32)
    return running

def attend_utterance(operands):
    query_rows, key_rows, value_rows, query_sum, key_mem, value_mem, length_one, bank_start = operands
    window = LC + SEG + RC
    head_count = D // HEAD_DIM
    key_padded = jnp.pad(key_rows, ((LC, RC), (0, 0)))
    value_padded = jnp.pad(value_rows, ((LC, RC), (0, 0)))
    bank_keys_padded = jnp.pad(key_mem, ((M, 0), (0, 0)))
    bank_values_padded = jnp.pad(value_mem, ((M, 0), (0, 0)))
    segment_ids = jnp.arange(SEGMENTS, dtype=jnp.int32)

    def one_segment(segment, bank_floor):
        seg_start = segment * SEG
        frame_keys = lax.dynamic_slice_in_dim(key_padded, seg_start, window, 0)
        frame_values = lax.dynamic_slice_in_dim(value_padded, seg_start, window, 0)
        bank_keys = lax.dynamic_slice_in_dim(bank_keys_padded, segment, M, 0)
        bank_values = lax.dynamic_slice_in_dim(bank_values_padded, segment, M, 0)
        row_block = jnp.concatenate([lax.dynamic_slice_in_dim(query_rows, seg_start, SEG, 0), lax.dynamic_slice_in_dim(query_sum, segment, 1, 0)], axis=0)
        all_keys = jnp.concatenate([frame_keys, bank_keys], axis=0)
        all_values = jnp.concatenate([frame_values, bank_values], axis=0)
        frame_pos = seg_start - LC + jnp.arange(window, dtype=jnp.int32)
        frame_ok = (frame_pos >= 0) & (frame_pos < length_one)
        bank_index = segment - M + jnp.arange(M, dtype=jnp.int32)
        bank_ok = (bank_index >= bank_floor) & (bank_index <= segment - 1)
        allowed = jnp.concatenate([frame_ok, bank_ok])
        query_heads = row_block.astype(jnp.float32).reshape(SEG + 1, head_count, HEAD_DIM)
        key_heads = all_keys.astype(jnp.float32).reshape(-1, head_count, HEAD_DIM)
        value_heads = all_values.astype(jnp.float32).reshape(-1, head_count, HEAD_DIM)
        scores = jnp.einsum('qhd,khd->hqk', query_heads, key_heads) * HEAD_DIM ** (-0.5)
        weights = jnp.where(allowed[None, None, :], jnp.exp(scores), 0.0)
        shares = (weights / lax.optimization_barrier(jnp.sum(weights, axis=-1, keepdims=True))).astype(jnp.bfloat16)
        mixture = jnp.einsum('hqk,khd->qhd', shares.astype(jnp.float32), value_heads)
        return mixture.reshape(SEG + 1, D).astype(jnp.bfloat16)
    outputs = jax.vmap(one_segment)(segment_ids, bank_start)
    frame_context = outputs[:, :SEG].reshape(FRAMES, D)
    summary_context = outputs[:, SEG]
    return (frame_context, summary_context)

def reference(filterbank, lengths, bank_begin, memory_in, w_front, gain_attn, w_query, w_key, w_value, w_out, gain_ffn, w_up, w_down):
    stacked = filterbank.reshape(UTT, FRAMES, STACK * FBANK)
    positions = jnp.arange(FRAMES, dtype=jnp.int32)
    valid_frame = positions[None, :] < lengths[:, None]
    front_out = product(stacked, w_front)
    inputs = jnp.where(valid_frame[:, :, None], front_out, 0.0).astype(jnp.bfloat16)
    summary = lax.optimization_barrier(jnp.mean(inputs.astype(jnp.float32).reshape(UTT, SEGMENTS, SEG, D), axis=2))
    normed = normalize(inputs.astype(jnp.float32), gain_attn).astype(jnp.bfloat16)
    normed_sum = normalize(summary, gain_attn).astype(jnp.bfloat16)
    normed_mem = normalize(memory_in.astype(jnp.float32), gain_attn).astype(jnp.bfloat16)
    queries = product(normed, w_query).astype(jnp.bfloat16)
    key_rows = product(normed, w_key).astype(jnp.bfloat16)
    value_rows = product(normed, w_value).astype(jnp.bfloat16)
    query_sum = product(normed_sum, w_query).astype(jnp.bfloat16)
    key_mem = product(normed_mem, w_key).astype(jnp.bfloat16)
    value_mem = product(normed_mem, w_value).astype(jnp.bfloat16)
    frame_context, summary_context = lax.map(attend_utterance, (queries, key_rows, value_rows, query_sum, key_mem, value_mem, lengths, bank_begin))
    attention = grouped_product(frame_context, w_out)
    memory = grouped_product(summary_context, w_out)
    hidden_in = (inputs.astype(jnp.float32) + attention).astype(jnp.bfloat16)
    seg_first = jnp.arange(SEGMENTS, dtype=jnp.int32) * SEG
    valid_seg = seg_first[None, :] < lengths[:, None]
    memory_out = jnp.where(valid_seg[:, :, None], memory, 0.0).astype(jnp.bfloat16)
    normed_ffn = normalize(hidden_in.astype(jnp.float32), gain_ffn).astype(jnp.bfloat16)
    hidden = jax.nn.gelu(product(normed_ffn, w_up)).astype(jnp.bfloat16)
    feed_out = grouped_product(hidden, w_down)
    encoded = jnp.where(valid_frame[:, :, None], hidden_in.astype(jnp.float32) + feed_out, 0.0).astype(jnp.bfloat16)
    return (encoded, memory_out)
```

```python
import jax
import jax.numpy as jnp
from jax import lax
from jax.experimental import pallas as pl
from jax.experimental.pallas import tpu as pltpu
from jax.sharding import PartitionSpec as P


D = 1024
HALF = 512
SEG = 4
LC = 32
RC = 4
M = 32
NX, NZ, NY, NC = 4, 4, 4, 2
TM = NX * NZ * NY * NC
U = 2
F = 256
S = 64
EXT = 320
QB, KB = 160, 256
KF = 192
epsilon = 1e-05
bf16, f32, i32 = jnp.bfloat16, jnp.float32, jnp.int32
AXES = ("tm", "mp")


def place(x, z, y, c, m):
    return ((((x % NX) * NZ + z) * NY + y % NY) * NC + c % NC) * 2 + m % 2


def route(step):
    dx, dy, dc, dm = step
    return [
        (place(x, z, y, c, m), place(x + dx, z, y + dy, c + dc, m + dm))
        for x in range(NX)
        for z in range(NZ)
        for y in range(NY)
        for c in range(NC)
        for m in range(2)
    ]


STEPS = {
    ("x", 1): (1, 0, 0, 0),
    ("x", -1): (-1, 0, 0, 0),
    ("y", 1): (0, 1, 0, 0),
    ("y", -1): (0, -1, 0, 0),
    ("c", 1): (0, 0, 1, 0),
    ("m", 1): (0, 0, 0, 1),
}


def moved(array, axis, by=1):
    return lax.ppermute(array, AXES, route(STEPS[axis, by]))


def along_frames(array, by):
    pairs = [
        (t * 2 + m, (t + by) * 2 + m) for t in range(TM) for m in range(2) if 0 <= t + by < TM
    ]
    return lax.ppermute(array, AXES, pairs)


def after(value, *earlier):
    return lax.optimization_barrier((value, *earlier))[0]


def first_ring(array, axis, way):
    one = moved(array, axis, way)
    return jnp.stack([array, one, moved(array, axis, -way), moved(one, axis, way)])


def far_ring(back, front, axis, way):
    return [moved(back[:2], axis, -way), moved(front[2:], axis, way)]


def partners(blocks):
    return [moved(b, "c") for b in blocks]


def each_piece(first, way, where):
    x, y, c = where
    near = (0, -way, way, -2 * way)
    far = ((0, 0, 4), (way, 0, 4), (-way, 0, 4), (2, 0, 2), (2, 2, 4))
    for i, (a2, low, high) in enumerate(far):
        for j in range(low, high):
            a1 = near[j]
            px = (x + (a1 if first == "x" else a2)) & 3
            py = (y + (a2 if first == "x" else a1)) & 3
            for k in range(2):
                pc = c if k == 0 else 1 - c
                yield i + 5 * k, j - low, px * 8 + py * 2 + pc


def dot(a, b):
    return jnp.dot(a, b, preferred_element_type=f32)


def normed(values, gain):
    center = jnp.sum(values, axis=-1, keepdims=True) * (1.0 / D)
    shifted = values - center
    spread_ = jnp.sum(shifted * shifted, axis=-1, keepdims=True) * (1.0 / D)
    return shifted * lax.rsqrt(spread_ + epsilon) * gain


def gelu(v):
    inner = 0.7978845608028654 * (v + 0.044715 * (v * v * v))
    return 0.5 * v * (1.0 + jnp.tanh(inner))


def pack_kernel(sc, wq, wk, wv, wo, wu, wd, s1, s23):
    s1[:32] = wq[...]
    s1[32:64] = wk[...]
    s1[64:96] = wv[...]
    s1[96:112] = wo[:, :HALF]
    s1[112:] = wo[:, HALF:]
    s23[:32] = wu[:, :D]
    s23[32:64] = wu[:, D:]
    s23[64:] = wd[...]


def front_kernel(
    sc, fb, left, right, wf_own, wf_a, wf_b, gain, wq, wk, wv, x_out, n_out, q, k, v, xs, fbs
):
    u = pl.program_id(0)
    h, c = sc[2], sc[5]
    fbs[:LC] = left[0]
    fbs[LC : LC + F] = fb[0]
    fbs[LC + F : LC + F + 16] = right[0]
    fbs[LC + F + 16 :] = jnp.zeros((16, 320), bf16)
    rows = fbs[...]
    pos = sc[3] * F - LC + lax.broadcasted_iota(i32, (EXT, 1), 0)
    valid = pos < sc[u]

    def put(at, width, w):
        part = jnp.where(valid, dot(rows, w[...]), 0.0).astype(bf16)
        xs[:, pl.ds(pl.multiple_of(at, 256), width)] = part

    other = (1 - h) * HALF
    put(h * HALF, HALF, wf_own)
    put(other + c * 256, 256, wf_a)
    put(other + (1 - c) * 256, 256, wf_b)
    x_out[0] = xs[LC : LC + F, :]
    g = gain[...]
    n_out[0, :EXT, :] = normed(xs[...].astype(f32), g).astype(bf16)
    seg = lax.broadcasted_iota(i32, (S, F), 0)
    frame = lax.broadcasted_iota(i32, (S, F), 1)
    pool = jnp.where(frame // SEG == seg, 0.25, 0.0).astype(bf16)
    n_out[0, EXT:, :] = normed(dot(pool, xs[LC : LC + F, :]), g).astype(bf16)
    project(n_out, wq, wk, wv, q, k, v)


def project(n, wq, wk, wv, q, k, v):
    q[0, :F, :] = (dot(n[0, LC : LC + F, :], wq[...]) * 0.125).astype(bf16)
    q[0, F:, :] = (dot(n[0, EXT:, :], wq[...]) * 0.125).astype(bf16)
    k[0] = dot(n[0, :EXT, :], wk[...]).astype(bf16)
    v[0] = dot(n[0, :EXT, :], wv[...]).astype(bf16)


def mask_of(sc, u, b, begins):
    t = sc[3]
    shape = (QB, S)
    r = lax.broadcasted_iota(i32, shape, 0)
    col = lax.broadcasted_iota(i32, shape, 1)
    local = 32 * b + jnp.where(r < 128, r // SEG, r - 128)
    begin = begins[pl.ds(2 * sc[2] + u, 1), :]
    floor = jnp.sum(jnp.where(col == local, begin, 0), axis=-1, keepdims=True)
    r = lax.broadcasted_iota(i32, (QB, 1), 0)
    seg = t * S + 32 * b + jnp.where(r < 128, r // SEG, r - 128)
    k = lax.broadcasted_iota(i32, (QB, KB), 1)
    pos = t * F - LC + 128 * b + k
    bank = t * S - M + 32 * b + k - KF
    low = jnp.maximum(seg * SEG - LC, 0)
    high = jnp.minimum((seg + 1) * SEG + RC, sc[u])
    sees_frame = (k < KF) & (pos >= low) & (pos < high)
    sees_bank = (k >= KF) & (bank >= floor) & (bank <= seg - 1)
    return jnp.where(sees_frame | sees_bank, 0.0, -1e30).astype(f32)


def attend(sc, u, begins, q, k, v, mk, mv, ctx):
    low = lax.broadcasted_iota(i32, (1, 128), 1) < 64
    for b in range(2):
        mask = mask_of(sc, u, b, begins)
        for p in range(4):
            lanes = slice(128 * p, 128 * p + 128)
            fr, sm = slice(128 * b, 128 * b + 128), slice(F + 32 * b, F + 32 * b + 32)
            kr, mr = slice(128 * b, 128 * b + KF), slice(32 * b, 32 * b + 64)
            qb = jnp.concatenate([q[0, fr, lanes], q[0, sm, lanes]], axis=0)
            zero = jnp.zeros_like(qb)
            pair = jnp.concatenate([jnp.where(low, qb, zero), jnp.where(low, zero, qb)], axis=0)
            keys = jnp.concatenate([k[0, kr, lanes], mk[mr, lanes]], axis=0)
            values = jnp.concatenate([v[0, kr, lanes], mv[mr, lanes]], axis=0)
            scores = lax.dot_general(
                pair, keys, (((1,), (1,)), ((), ())), preferred_element_type=f32
            )
            weights = jnp.exp(scores + jnp.concatenate([mask, mask], axis=0))
            total = jnp.sum(weights, axis=-1, keepdims=True)
            shares = (weights * (1.0 / total)).astype(bf16)
            mixed = dot(shares, values)
            part = jnp.where(low, mixed[:QB], mixed[QB:]).astype(bf16)
            ctx[0, fr, lanes] = part[:128]
            ctx[0, sm, lanes] = part[128:]


def own_heads_kernel(
    sc, mem_a, mem_b, halo_a, halo_b, begins, gain, wk, wv, q, k, v, ctx, nm, mk, mv, ms
):
    h = sc[2]
    for start, halo, mem in ((h, halo_a, mem_a), (1 - h, halo_b, mem_b)):
        cols = pl.ds(pl.multiple_of(start * HALF, HALF), HALF)
        ms[:M, cols] = halo[0]
        ms[M:, cols] = mem[0]
    nm[0] = normed(ms[...].astype(f32), gain[...]).astype(bf16)
    mk[...] = dot(nm[0], wk[...]).astype(bf16)
    mv[...] = dot(nm[0], wv[...]).astype(bf16)
    attend(sc, pl.program_id(0), begins, q, k, v, mk, mv, ctx)


def other_heads_kernel(*refs):
    sc, n, nm, begins, ctx_own, x, wo_own, gain = refs[:8]
    parts = refs[8:18]
    hid, nf, memory = refs[18:21]
    wq, wk, wv, wo, q, k, v, mk, mv, ctx, sem = refs[21:]
    u = pl.program_id(0)

    def ready(i, w):
        @pl.when(u == 0)
        def _():
            pltpu.make_async_copy(w, w, sem.at[i]).wait()

    @pl.when(u == 0)
    def _():
        for part in range(4):
            for r, j, at in each_piece("y", -1, (sc[4], sc[6], sc[5])):
                rows = pl.ds(pl.multiple_of(at * 32, 32), 32)
                few = pl.ds(pl.multiple_of(at * 16, 16), 16)
                if part < 3:
                    w = (wk, wv, wq)[part]
                    lo = (32, 64, 0)[part]
                    src = parts[r].at[j, lo : lo + 32]
                    pltpu.make_async_copy(src, w.at[rows], sem.at[part]).start()
                else:
                    for s in range(2):
                        src = parts[r].at[j, 96 + 16 * s : 112 + 16 * s]
                        dst = wo.at[few, HALF * s : HALF * s + HALF]
                        pltpu.make_async_copy(src, dst, sem.at[3]).start()

    mine = dot(ctx_own[0], wo_own[...]).astype(bf16).astype(f32)
    ready(0, wk)
    k[0] = dot(n[0, :EXT, :], wk[...]).astype(bf16)
    mk[...] = dot(nm[0], wk[...]).astype(bf16)
    ready(1, wv)
    v[0] = dot(n[0, :EXT, :], wv[...]).astype(bf16)
    mv[...] = dot(nm[0], wv[...]).astype(bf16)
    ready(2, wq)
    q[0, :F, :] = (dot(n[0, LC : LC + F, :], wq[...]) * 0.125).astype(bf16)
    q[0, F:, :] = (dot(n[0, EXT:, :], wq[...]) * 0.125).astype(bf16)
    attend(sc, u, begins, q, k, v, mk, mv, ctx)
    ready(3, wo)
    theirs = dot(ctx[0], wo[...]).astype(bf16).astype(f32)
    both = mine + theirs
    seg = sc[3] * S + lax.broadcasted_iota(i32, (S, 1), 0)
    memory[0] = jnp.where(seg * SEG < sc[u], both[F:], 0.0).astype(bf16)
    residual = (x[0].astype(f32) + both[:F]).astype(bf16)
    hid[0] = residual
    nf[0] = normed(residual.astype(f32), gain[...]).astype(bf16)


def own_hidden_kernel(nf, wu, wd, out, acc):
    j = pl.program_id(0)
    hidden = gelu(dot(nf[...], wu[...])).astype(bf16)
    part = dot(hidden, wd[...])

    @pl.when(j == 0)
    def _():
        acc[...] = part

    @pl.when(j > 0)
    def _():
        acc[...] += part

    @pl.when(j == pl.num_programs(0) - 1)
    def _():
        out[...] = acc[...].astype(bf16)


def other_hidden_kernel(*refs):
    sc, nf, hid, own = refs[:4]
    parts = refs[4:14]
    out_own, out_other = refs[14:16]
    wu, wd, acc, sem = refs[16:]
    where = (sc[4], sc[6], sc[5])

    def fetch_up(i):
        for r, j, at in each_piece("x", 1, where):
            rows = pl.ds(pl.multiple_of(at * 32, 32), 32)
            lo, col = 32 * (i // 2), HALF * (i % 2)
            src = parts[r].at[j, lo : lo + 32, col : col + HALF]
            pltpu.make_async_copy(src, wu.at[i, rows], sem.at[i]).start()

    fetch_up(0)
    for r, j, at in each_piece("x", 1, where):
        rows = pl.ds(pl.multiple_of(at * 64, 64), 64)
        pltpu.make_async_copy(parts[r].at[j, 64:], wd.at[rows], sem.at[4]).start()
    for i in range(1, 4):
        fetch_up(i)
    for i in range(4):
        pltpu.make_async_copy(wu.at[i], wu.at[i], sem.at[i]).wait()
        hidden = gelu(dot(nf[...], wu[i])).astype(bf16)
        if i == 0:
            pltpu.make_async_copy(wd, wd, sem.at[4]).wait()
            acc[...] = dot(hidden, wd[:HALF])
        else:
            acc[...] += dot(hidden, wd[HALF * i : HALF * i + HALF])
    h = sc[2]
    row = lax.broadcasted_iota(i32, (F, 1), 0)
    for u in range(U):
        valid = sc[3] * F + row < sc[u]
        at = slice(F * u, F * u + F)
        for out, start in ((out_own, h * HALF), (out_other, (1 - h) * HALF)):
            cols = pl.ds(pl.multiple_of(start, HALF), HALF)
            feed = own[at, cols].astype(f32) + acc[at, cols].astype(bf16).astype(f32)
            whole = hid[at, cols].astype(f32) + feed
            out[u] = jnp.where(valid, whole, 0.0).astype(bf16)


def one(shape):
    return pl.BlockSpec((1,) + shape, lambda u, *_: (u,) + (0,) * len(shape))


def all_of(shape):
    return pl.BlockSpec(shape, lambda *_: (0,) * len(shape))


ANY = pl.BlockSpec(memory_space=pl.ANY)


def arrays(*shapes):
    return [jax.ShapeDtypeStruct(s, bf16) for s in shapes]


def call(kernel, grid, ins, outs, out_shape, scratch, flops, args, scalars=None):
    spec = pltpu.PrefetchScalarGridSpec(
        num_scalar_prefetch=0 if scalars is None else 1,
        grid=grid,
        in_specs=ins,
        out_specs=outs,
        scratch_shapes=scratch,
    )
    given = list(args) if scalars is None else [scalars, *args]
    return pl.pallas_call(
        kernel,
        grid_spec=spec,
        out_shape=out_shape,
        compiler_params=pltpu.CompilerParams(
            dimension_semantics=("arbitrary",) * len(grid), vmem_limit_bytes=48 << 20
        ),
        cost_estimate=pl.CostEstimate(
            flops=flops, bytes_accessed=8 << 20, transcendentals=1 << 20
        ),
    )(*given)


def cut(array, at, size, dim):
    return lax.dynamic_slice_in_dim(array, at, size, dim)


def joined(own, other, h, dim):
    return jnp.where(
        h == 0,
        jnp.concatenate([own, other], axis=dim),
        jnp.concatenate([other, own], axis=dim),
    )


def body(
    filterbank,
    lengths,
    bank_begin,
    memory_in,
    w_front,
    gain_attn,
    w_query,
    w_key,
    w_value,
    w_out,
    gain_ffn,
    w_up,
    w_down,
):
    t, h = lax.axis_index("tm"), lax.axis_index("mp")
    x_at, y_at, c_at = t // (NZ * NY * NC), (t // NC) % NY, t % NC
    piece = x_at * 8 + y_at * 2 + c_at
    lens = cut(lengths, 2 * h, 2, 0)
    scalars = jnp.concatenate([lens, jnp.stack([h, t, x_at, c_at, y_at, piece]).astype(i32)])

    gain_a, gain_f = gain_attn.reshape(1, D), gain_ffn.reshape(1, D)

    wf_cut = cut(w_front, c_at * 256, 256, 1)
    wf_a = moved(wf_cut, "m")
    wf_b = moved(wf_a, "c")

    def piece_of(rows, width):
        return pl.BlockSpec((rows, width), lambda i, sc: (sc[7], 0))

    s1, s23 = call(
        pack_kernel,
        (1,),
        [piece_of(32, HALF)] * 3 + [piece_of(16, D), piece_of(32, 2048), piece_of(64, D)],
        [all_of((128, HALF)), all_of((128, D))],
        arrays((128, HALF), (128, D)),
        [],
        1 << 20,
        (w_query, w_key, w_value, w_out, w_up, w_down),
        after(scalars, wf_cut),
    )
    filterbank = after(filterbank, s1)
    s23 = moved(s23, "m")
    s1 = moved(s1, "m")
    mem_other = moved(cut(memory_in, 2 * (1 - h), 2, 0), "m")

    fb = filterbank.reshape(4, F, 320)
    mine = cut(fb, 2 * h, 2, 0)
    left = along_frames(mine[:, F - LC :], 1)
    right = along_frames(mine[:, :16], -1)
    halo_own = along_frames(cut(memory_in, 2 * h, 2, 0)[:, S - M :], 1)

    x, n, q, kk, v = call(
        front_kernel,
        (U,),
        [pl.BlockSpec((1, F, 320), lambda u, sc: (2 * sc[2] + u, 0, 0))]
        + [one((LC, 320)), one((16, 320))]
        + [all_of((320, HALF)), all_of((320, 256)), all_of((320, 256))]
        + [all_of((1, D))]
        + [all_of((D, HALF))] * 3,
        [one((F, D)), one((EXT + S, D))] + [one((EXT, HALF))] * 3,
        arrays((U, F, D), (U, EXT + S, D), *[(U, EXT, HALF)] * 3),
        [pltpu.VMEM((EXT, D), bf16), pltpu.VMEM((EXT, 320), bf16)],
        2 * 640 * 1024 * 1536,
        (fb, left, right, w_front, wf_a, wf_b, gain_a, w_query, w_key, w_value),
        scalars,
    )
    s1, s23, mem_other = after(s1, x), after(s23, x), after(mem_other, x)
    halo_other = along_frames(mem_other[:, S - M :], 1)
    filled1 = first_ring(s1, "y", -1)
    back1, front1 = moved(filled1, "x", 1), moved(filled1, "x", -1)
    filled23 = first_ring(s23, "x", 1)
    back23, front23 = moved(filled23, "y", -1), moved(filled23, "y", 1)
    ctx, nm = call(
        own_heads_kernel,
        (U,),
        [pl.BlockSpec((1, S, HALF), lambda u, sc: (2 * sc[2] + u, 0, 0)), one((S, HALF))]
        + [one((M, HALF))] * 2
        + [all_of((4, S)), all_of((1, D)), all_of((D, HALF)), all_of((D, HALF))]
        + [one((EXT, HALF))] * 3,
        [one((EXT, HALF)), one((S + M, D))],
        arrays((U, EXT, HALF), (U, S + M, D)),
        [pltpu.VMEM((S + M, HALF), bf16)] * 2 + [pltpu.VMEM((S + M, D), bf16)],
        2 << 30,
        (memory_in, mem_other, halo_own, halo_other, bank_begin, gain_a, w_key, w_value, q, kk, v),
        scalars,
    )
    back1, front1, filled1 = lax.optimization_barrier((back1, front1, filled1, ctx))[:3]
    blocks1 = [filled1, back1, front1] + far_ring(back1, front1, "x", -1)
    blocks1 += partners(blocks1)
    hid, nf, memory = call(
        other_heads_kernel,
        (U,),
        [one((EXT + S, D)), one((S + M, D)), all_of((4, S)), one((EXT, HALF)), one((F, D))]
        + [all_of((HALF, D)), all_of((1, D))]
        + [ANY] * 10,
        [one((F, D)), one((F, D)), one((S, D))],
        arrays((U, F, D), (U, F, D), (U, S, D)),
        [pltpu.VMEM((D, HALF), bf16)] * 3
        + [pltpu.VMEM((HALF, D), bf16)]
        + [pltpu.VMEM((1, EXT, HALF), bf16)] * 3
        + [pltpu.VMEM((S + M, HALF), bf16)] * 2
        + [pltpu.VMEM((1, EXT, HALF), bf16), pltpu.SemaphoreType.DMA((4,))],
        6 << 30,
        (n, nm, bank_begin, ctx, x, w_out, gain_f, *blocks1),
        scalars,
    )
    back23, front23, filled23 = lax.optimization_barrier((back23, front23, filled23, hid))[:3]
    blocks23 = [filled23, back23, front23] + far_ring(back23, front23, "y", 1)
    near23 = partners(blocks23[:3])
    memory_other = moved(cut(memory, (1 - h) * HALF, HALF, 2), "m")
    rows = U * F
    nf, hid = nf.reshape(rows, D), hid.reshape(rows, D)
    own = call(
        own_hidden_kernel,
        (4,),
        [
            all_of((rows, D)),
            pl.BlockSpec((D, HALF), lambda j: (0, j)),
            pl.BlockSpec((HALF, D), lambda j: (j, 0)),
        ],
        all_of((rows, D)),
        arrays((rows, D))[0],
        [pltpu.VMEM((rows, D), f32)],
        4 << 30,
        (nf, w_up, w_down),
        None,
    )
    far23 = partners([after(b, own) for b in blocks23[3:]])
    blocks23 += near23 + far23
    memory_other, hid = lax.optimization_barrier((memory_other, hid))
    out_own, out_other = call(
        other_hidden_kernel,
        (1,),
        [all_of((rows, D))] * 3 + [ANY] * 10,
        [all_of((U, F, HALF))] * 2,
        arrays((U, F, HALF), (U, F, HALF)),
        [
            pltpu.VMEM((4, D, HALF), bf16),
            pltpu.VMEM((2048, D), bf16),
            pltpu.VMEM((rows, D), f32),
            pltpu.SemaphoreType.DMA((5,)),
        ],
        4 << 30,
        (nf, hid, own, *blocks23),
        scalars,
    )
    memory_out = joined(cut(memory, h * HALF, HALF, 2), memory_other, h, 0)
    encoded = joined(out_own, moved(out_other, "m"), h, 0)
    return encoded, memory_out


def solution(mesh):
    in_specs = (
        P(None, "tm", None),
        P(),
        P(None, "tm"),
        P(None, "tm", "mp"),
        P(None, "mp"),
        P(),
        P(None, "mp"),
        P(None, "mp"),
        P(None, "mp"),
        P("mp", None),
        P(),
        P(None, "mp"),
        P("mp", None),
    )
    out_specs = (P(None, "tm", "mp"), P(None, "tm", "mp"))

    return jax.shard_map(
        body, mesh=mesh, in_specs=in_specs, out_specs=out_specs, check_vma=False
    )
```

```python
import jax
import jax.numpy as jnp
from jax import lax
from jax.experimental import pallas as pl
from jax.experimental.pallas import tpu as pltpu
from jax.sharding import PartitionSpec as P


D = 1024
HALF = 512
SEG = 4
LC = 32
RC = 4
M = 32
NX, NZ, NY, NC = 4, 4, 4, 2
TM = NX * NZ * NY * NC
U = 2
F = 256
S = 64
EXT = 320
QB, KB = 160, 256
KF = 192
epsilon = 1e-05
bf16, f32, i32 = jnp.bfloat16, jnp.float32, jnp.int32
AXES = ("tm", "mp")
GRANTS = {
    "pack": 60,
    "pack_ffn": 60,
    "front": 30,
    "own_heads": 24,
    "other_heads": 30,
    "own_hidden": 24,
    "other_hidden": 36,
}


def place(x, z, y, c, m):
    return ((((x % NX) * NZ + z) * NY + y % NY) * NC + c % NC) * 2 + m % 2


def route(step):
    dx, dy, dc, dm = step
    return [
        (place(x, z, y, c, m), place(x + dx, z, y + dy, c + dc, m + dm))
        for x in range(NX)
        for z in range(NZ)
        for y in range(NY)
        for c in range(NC)
        for m in range(2)
    ]


STEPS = {
    ("x", 1): (1, 0, 0, 0),
    ("x", -1): (-1, 0, 0, 0),
    ("y", 1): (0, 1, 0, 0),
    ("y", -1): (0, -1, 0, 0),
    ("c", 1): (0, 0, 1, 0),
    ("m", 1): (0, 0, 0, 1),
}


def moved(array, axis, by=1):
    return lax.ppermute(array, AXES, route(STEPS[axis, by]))


def along_frames(array, by):
    pairs = [
        (t * 2 + m, (t + by) * 2 + m) for t in range(TM) for m in range(2) if 0 <= t + by < TM
    ]
    return lax.ppermute(array, AXES, pairs)


def after(value, *earlier):
    return lax.optimization_barrier((value, *earlier))[0]


def both_ways(array, axis, way):
    back = moved(array, axis, way)
    front = moved(array, axis, -way)
    return back, front


def partners(blocks):
    return [moved(b, "c") for b in blocks]


def each_piece(first, way, where, halves):
    x, y, c = where
    near = (0, -way, way, -2 * way)
    far = [(0, 0, 4), (way, 0, 4), (-way, 0, 4)]
    far += [(2, 0, 2), (2, 2, 4)] if halves else [(2, 0, 4)]
    for i, (a2, low, high) in enumerate(far):
        for j in range(low, high):
            a1 = near[j]
            px = (x + (a1 if first == "x" else a2)) & 3
            py = (y + (a2 if first == "x" else a1)) & 3
            for k in range(2):
                pc = c if k == 0 else 1 - c
                yield i + len(far) * k, j - low, px * 8 + py * 2 + pc


def dot(a, b):
    return jnp.dot(a, b, preferred_element_type=f32)


def normed(values, gain):
    center = jnp.sum(values, axis=-1, keepdims=True) * (1.0 / D)
    shifted = values - center
    spread_ = jnp.sum(shifted * shifted, axis=-1, keepdims=True) * (1.0 / D)
    return shifted * lax.rsqrt(spread_ + epsilon) * gain


def gelu(v):
    inner = 0.7978845608028654 * (v + 0.044715 * (v * v * v))
    return 0.5 * v * (1.0 + jnp.tanh(inner))


def pack_kernel(sc, wq, wk, wv, wo, s1):
    s1[:, :HALF] = wq[...]
    s1[:, HALF : 2 * HALF] = wk[...]
    s1[:, 2 * HALF : 3 * HALF] = wv[...]
    s1[:16, 3 * HALF :] = wo[:, :HALF]
    s1[16:, 3 * HALF :] = wo[:, HALF:]


def pack_ffn_kernel(sc, wu, wd, up, down):
    up[...] = wu[...]
    down[...] = wd[...]


def front_kernel(
    sc, fb, left, right, wf_own, wf_a, wf_b, gain, wq, wk, wv, x_out, n_out, q, k, v, xs, fbs
):
    u = pl.program_id(0)
    h, c = sc[2], sc[5]
    fbs[:LC] = left[0]
    fbs[LC : LC + F] = fb[0]
    fbs[LC + F : LC + F + 16] = right[0]
    fbs[LC + F + 16 :] = jnp.zeros((16, 320), bf16)
    rows = fbs[...]
    pos = sc[3] * F - LC + lax.broadcasted_iota(i32, (EXT, 1), 0)
    valid = pos < sc[u]

    def put(at, width, w):
        part = jnp.where(valid, dot(rows, w[...]), 0.0).astype(bf16)
        xs[:, pl.ds(pl.multiple_of(at, 256), width)] = part

    other = (1 - h) * HALF
    put(h * HALF, HALF, wf_own)
    put(other + c * 256, 256, wf_a)
    put(other + (1 - c) * 256, 256, wf_b)
    x_out[0] = xs[LC : LC + F, :]
    g = gain[...]
    n_out[0, :EXT, :] = normed(xs[...].astype(f32), g).astype(bf16)
    seg = lax.broadcasted_iota(i32, (S, F), 0)
    frame = lax.broadcasted_iota(i32, (S, F), 1)
    pool = jnp.where(frame // SEG == seg, 0.25, 0.0).astype(bf16)
    n_out[0, EXT:, :] = normed(dot(pool, xs[LC : LC + F, :]), g).astype(bf16)
    project(n_out, wq, wk, wv, q, k, v)


def project(n, wq, wk, wv, q, k, v):
    q[0, :F, :] = (dot(n[0, LC : LC + F, :], wq[...]) * 0.125).astype(bf16)
    q[0, F:, :] = (dot(n[0, EXT:, :], wq[...]) * 0.125).astype(bf16)
    k[0] = dot(n[0, :EXT, :], wk[...]).astype(bf16)
    v[0] = dot(n[0, :EXT, :], wv[...]).astype(bf16)


def mask_of(sc, u, b, begins):
    t = sc[3]
    shape = (QB, S)
    r = lax.broadcasted_iota(i32, shape, 0)
    col = lax.broadcasted_iota(i32, shape, 1)
    local = 32 * b + jnp.where(r < 128, r // SEG, r - 128)
    begin = begins[pl.ds(2 * sc[2] + u, 1), :]
    floor = jnp.sum(jnp.where(col == local, begin, 0), axis=-1, keepdims=True)
    r = lax.broadcasted_iota(i32, (QB, 1), 0)
    seg = t * S + 32 * b + jnp.where(r < 128, r // SEG, r - 128)
    k = lax.broadcasted_iota(i32, (QB, KB), 1)
    pos = t * F - LC + 128 * b + k
    bank = t * S - M + 32 * b + k - KF
    low = jnp.maximum(seg * SEG - LC, 0)
    high = jnp.minimum((seg + 1) * SEG + RC, sc[u])
    sees_frame = (k < KF) & (pos >= low) & (pos < high)
    sees_bank = (k >= KF) & (bank >= floor) & (bank <= seg - 1)
    return jnp.where(sees_frame | sees_bank, 0.0, -1e30).astype(f32)


def attend(sc, u, begins, q, k, v, mk, mv, ctx):
    low = lax.broadcasted_iota(i32, (1, 128), 1) < 64

    def block(b, carry):
        mask = mask_of(sc, u, b, begins)
        masks = jnp.concatenate([mask, mask], axis=0)
        at = pl.multiple_of(b * 128, 128)
        few = pl.multiple_of(b * 32, 32)
        fr, sm = pl.ds(at, 128), pl.ds(F + few, 32)
        kr, mr = pl.ds(at, KF), pl.ds(few, 64)
        for p in range(4):
            lanes = slice(128 * p, 128 * p + 128)
            qb = jnp.concatenate([q[0, fr, lanes], q[0, sm, lanes]], axis=0)
            zero = jnp.zeros_like(qb)
            pair = jnp.concatenate([jnp.where(low, qb, zero), jnp.where(low, zero, qb)], axis=0)
            keys = jnp.concatenate([k[0, kr, lanes], mk[mr, lanes]], axis=0)
            values = jnp.concatenate([v[0, kr, lanes], mv[mr, lanes]], axis=0)
            scores = lax.dot_general(
                pair, keys, (((1,), (1,)), ((), ())), preferred_element_type=f32
            )
            weights = jnp.exp(scores + masks)
            total = jnp.sum(weights, axis=-1, keepdims=True)
            shares = (weights * (1.0 / total)).astype(bf16)
            mixed = dot(shares, values)
            part = jnp.where(low, mixed[:QB], mixed[QB:]).astype(bf16)
            ctx[0, fr, lanes] = part[:128]
            ctx[0, sm, lanes] = part[128:]
        return carry

    lax.fori_loop(0, 2, block, 0)


def own_heads_kernel(
    sc, mem_a, mem_b, halo_a, halo_b, begins, gain, wk, wv, q, k, v, ctx, nm, mk, mv, ms
):
    h = sc[2]
    for start, halo, mem in ((h, halo_a, mem_a), (1 - h, halo_b, mem_b)):
        cols = pl.ds(pl.multiple_of(start * HALF, HALF), HALF)
        ms[:M, cols] = halo[0]
        ms[M:, cols] = mem[0]
    nm[0] = normed(ms[...].astype(f32), gain[...]).astype(bf16)
    mk[...] = dot(nm[0], wk[...]).astype(bf16)
    mv[...] = dot(nm[0], wv[...]).astype(bf16)
    attend(sc, pl.program_id(0), begins, q, k, v, mk, mv, ctx)


def other_heads_kernel(*refs):
    sc, n, nm, begins, ctx_own, x, wo_own, gain = refs[:8]
    parts = refs[8:18]
    hid, nf, memory = refs[18:21]
    wqkv, wo, q, k, v, mk, mv, ctx, sem = refs[21:]
    u = pl.program_id(0)
    where = (sc[4], sc[6], sc[5])

    @pl.when(u == 0)
    def _():
        for r, j, at in each_piece("y", -1, where, True):
            rows = pl.ds(pl.multiple_of(at * 32, 32), 32)
            src = parts[r].at[j, :, : 3 * HALF]
            pltpu.make_async_copy(src, wqkv.at[rows], sem.at[0]).start()
        for r, j, at in each_piece("y", -1, where, True):
            few = pl.ds(pl.multiple_of(at * 16, 16), 16)
            for s in range(2):
                src = parts[r].at[j, 16 * s : 16 * s + 16, 3 * HALF :]
                dst = wo.at[few, HALF * s : HALF * s + HALF]
                pltpu.make_async_copy(src, dst, sem.at[1]).start()

    mine = dot(ctx_own[0], wo_own[...]).astype(bf16).astype(f32)

    @pl.when(u == 0)
    def _():
        pltpu.make_async_copy(wqkv, wqkv, sem.at[0]).wait()
        pltpu.make_async_copy(wo, wo, sem.at[1]).wait()

    wk, wv = wqkv.at[:, HALF : 2 * HALF], wqkv.at[:, 2 * HALF :]
    project(n, wqkv.at[:, :HALF], wk, wv, q, k, v)
    mk[...] = dot(nm[0], wk[...]).astype(bf16)
    mv[...] = dot(nm[0], wv[...]).astype(bf16)
    attend(sc, u, begins, q, k, v, mk, mv, ctx)
    theirs = dot(ctx[0], wo[...]).astype(bf16).astype(f32)
    both = mine + theirs
    seg = sc[3] * S + lax.broadcasted_iota(i32, (S, 1), 0)
    memory[0] = jnp.where(seg * SEG < sc[u], both[F:], 0.0).astype(bf16)
    residual = (x[0].astype(f32) + both[:F]).astype(bf16)
    hid[0] = residual
    nf[0] = normed(residual.astype(f32), gain[...]).astype(bf16)


def own_hidden_kernel(nf, wu, wd, out, acc):
    j = pl.program_id(0)
    hidden = gelu(dot(nf[...], wu[...])).astype(bf16)
    part = dot(hidden, wd[...])

    @pl.when(j == 0)
    def _():
        acc[...] = part

    @pl.when(j > 0)
    def _():
        acc[...] += part

    @pl.when(j == pl.num_programs(0) - 1)
    def _():
        out[...] = acc[...].astype(bf16)


def other_hidden_kernel(*refs):
    sc, nf, hid, own = refs[:4]
    ups, downs = refs[4:12], refs[12:20]
    out_own, out_other = refs[20:22]
    wu, wd, acc, sem = refs[22:]
    where = (sc[4], sc[6], sc[5])

    def fetch_up(i):
        for r, j, at in each_piece("x", 1, where, False):
            rows = pl.ds(pl.multiple_of(at * 32, 32), 32)
            src = ups[r].at[j, :, HALF * i : HALF * i + HALF]
            pltpu.make_async_copy(src, wu.at[i, rows], sem.at[i]).start()

    fetch_up(0)
    for r, j, at in each_piece("y", -1, where, False):
        rows = pl.ds(pl.multiple_of(at * 64, 64), 64)
        pltpu.make_async_copy(downs[r].at[j], wd.at[rows], sem.at[4]).start()
    for i in range(1, 4):
        fetch_up(i)

    def step(i, carry):
        pltpu.make_async_copy(wu.at[i], wu.at[i], sem.at[i]).wait()
        hidden = gelu(dot(nf[...], wu[i])).astype(bf16)

        @pl.when(i == 0)
        def _():
            pltpu.make_async_copy(wd, wd, sem.at[4]).wait()
            acc[...] = jnp.zeros_like(acc)

        acc[...] += dot(hidden, wd[pl.ds(pl.multiple_of(i * HALF, HALF), HALF)])
        return carry

    lax.fori_loop(0, 4, step, 0)
    h = sc[2]
    row = lax.broadcasted_iota(i32, (F, 1), 0)
    for u in range(U):
        valid = sc[3] * F + row < sc[u]
        at = slice(F * u, F * u + F)
        for out, start in ((out_own, h * HALF), (out_other, (1 - h) * HALF)):
            cols = pl.ds(pl.multiple_of(start, HALF), HALF)
            feed = own[at, cols].astype(f32) + acc[at, cols].astype(bf16).astype(f32)
            whole = hid[at, cols].astype(f32) + feed
            out[u] = jnp.where(valid, whole, 0.0).astype(bf16)


def one(shape):
    return pl.BlockSpec((1,) + shape, lambda u, *_: (u,) + (0,) * len(shape))


def all_of(shape):
    return pl.BlockSpec(shape, lambda *_: (0,) * len(shape))


ANY = pl.BlockSpec(memory_space=pl.ANY)


def arrays(*shapes):
    return [jax.ShapeDtypeStruct(s, bf16) for s in shapes]


def call(kernel, grid, ins, outs, out_shape, scratch, flops, args, scalars=None, name=None):
    spec = pltpu.PrefetchScalarGridSpec(
        num_scalar_prefetch=0 if scalars is None else 1,
        grid=grid,
        in_specs=ins,
        out_specs=outs,
        scratch_shapes=scratch,
    )
    given = list(args) if scalars is None else [scalars, *args]
    return pl.pallas_call(
        kernel,
        grid_spec=spec,
        out_shape=out_shape,
        compiler_params=pltpu.CompilerParams(
            dimension_semantics=("arbitrary",) * len(grid), vmem_limit_bytes=GRANTS[name] << 20
        ),
        cost_estimate=pl.CostEstimate(
            flops=flops, bytes_accessed=8 << 20, transcendentals=1 << 20
        ),
    )(*given)


def cut(array, at, size, dim):
    return lax.dynamic_slice_in_dim(array, at, size, dim)


def joined(own, other, h, dim):
    return jnp.where(
        h == 0,
        jnp.concatenate([own, other], axis=dim),
        jnp.concatenate([other, own], axis=dim),
    )


def body(
    filterbank,
    lengths,
    bank_begin,
    memory_in,
    w_front,
    gain_attn,
    w_query,
    w_key,
    w_value,
    w_out,
    gain_ffn,
    w_up,
    w_down,
):
    t, h = lax.axis_index("tm"), lax.axis_index("mp")
    x_at, y_at, c_at = t // (NZ * NY * NC), (t // NC) % NY, t % NC
    piece = x_at * 8 + y_at * 2 + c_at
    lens = cut(lengths, 2 * h, 2, 0)
    scalars = jnp.concatenate([lens, jnp.stack([h, t, x_at, c_at, y_at, piece]).astype(i32)])

    gain_a, gain_f = gain_attn.reshape(1, D), gain_ffn.reshape(1, D)

    wf_cut = cut(w_front, c_at * 256, 256, 1)
    wf_a = moved(wf_cut, "m")
    wf_b = moved(wf_a, "c")

    def piece_of(rows, width):
        return pl.BlockSpec((rows, width), lambda i, sc: (sc[7], 0))

    s1 = call(
        pack_kernel,
        (1,),
        [piece_of(32, HALF)] * 3 + [piece_of(16, D)],
        all_of((32, 2048)),
        arrays((32, 2048))[0],
        [],
        1 << 20,
        (w_query, w_key, w_value, w_out),
        after(scalars, wf_cut),
        "pack",
    )
    up, down = call(
        pack_ffn_kernel,
        (1,),
        [piece_of(32, 2048), piece_of(64, D)],
        [all_of((32, 2048)), all_of((64, D))],
        arrays((32, 2048), (64, D)),
        [],
        1 << 20,
        (w_up, w_down),
        after(scalars, s1),
        "pack_ffn",
    )
    filterbank = after(filterbank, up)
    s1 = moved(s1, "m")
    up = moved(up, "m")
    down = moved(down, "m")
    mem_other = moved(cut(memory_in, 2 * (1 - h), 2, 0), "m")
    back, front = both_ways(s1, "y", -1)
    filled1 = jnp.stack([s1, back, front, moved(back, "y", -1)])
    back1, front1 = both_ways(filled1, "x", 1)

    fb = filterbank.reshape(4, F, 320)
    mine = cut(fb, 2 * h, 2, 0)
    left = along_frames(mine[:, F - LC :], 1)
    right = along_frames(mine[:, :16], -1)
    halo_own = along_frames(cut(memory_in, 2 * h, 2, 0)[:, S - M :], 1)

    x, n, q, kk, v = call(
        front_kernel,
        (U,),
        [pl.BlockSpec((1, F, 320), lambda u, sc: (2 * sc[2] + u, 0, 0))]
        + [one((LC, 320)), one((16, 320))]
        + [all_of((320, HALF)), all_of((320, 256)), all_of((320, 256))]
        + [all_of((1, D))]
        + [all_of((D, HALF))] * 3,
        [one((F, D)), one((EXT + S, D))] + [one((EXT, HALF))] * 3,
        arrays((U, F, D), (U, EXT + S, D), *[(U, EXT, HALF)] * 3),
        [pltpu.VMEM((EXT, D), bf16), pltpu.VMEM((EXT, 320), bf16)],
        2 * 640 * 1024 * 1536,
        (fb, left, right, w_front, wf_a, wf_b, gain_a, w_query, w_key, w_value),
        scalars,
        "front",
    )
    up, down, mem_other = after(up, x), after(down, x), after(mem_other, x)
    halo_other = along_frames(mem_other[:, S - M :], 1)
    up_back, up_front = both_ways(up, "x", 1)
    down_back, down_front = both_ways(down, "y", -1)
    ctx, nm = call(
        own_heads_kernel,
        (U,),
        [pl.BlockSpec((1, S, HALF), lambda u, sc: (2 * sc[2] + u, 0, 0)), one((S, HALF))]
        + [one((M, HALF))] * 2
        + [all_of((4, S)), all_of((1, D)), all_of((D, HALF)), all_of((D, HALF))]
        + [one((EXT, HALF))] * 3,
        [one((EXT, HALF)), one((S + M, D))],
        arrays((U, EXT, HALF), (U, S + M, D)),
        [pltpu.VMEM((S + M, HALF), bf16)] * 2 + [pltpu.VMEM((S + M, D), bf16)],
        2 << 30,
        (memory_in, mem_other, halo_own, halo_other, bank_begin, gain_a, w_key, w_value, q, kk, v),
        scalars,
        "own_heads",
    )
    up_back, down_back = after(up_back, ctx), after(down_back, ctx)
    ups = jnp.stack([up, up_back, up_front, moved(up_back, "x", 1)])
    downs = jnp.stack([down, down_back, down_front, moved(down_back, "y", -1)])
    ups = [ups, *both_ways(ups, "y", -1)]
    downs = [downs, *both_ways(downs, "x", 1)]
    back1, front1, filled1 = after(back1, ctx), after(front1, ctx), after(filled1, ctx)
    blocks1 = [filled1, back1, front1]
    blocks1 += [moved(back1[:2], "x", 1), moved(front1[2:], "x", -1)]
    blocks1 += partners(blocks1)
    hid, nf, memory = call(
        other_heads_kernel,
        (U,),
        [one((EXT + S, D)), one((S + M, D)), all_of((4, S)), one((EXT, HALF)), one((F, D))]
        + [all_of((HALF, D)), all_of((1, D))]
        + [ANY] * 10,
        [one((F, D)), one((F, D)), one((S, D))],
        arrays((U, F, D), (U, F, D), (U, S, D)),
        [pltpu.VMEM((D, 3 * HALF), bf16), pltpu.VMEM((HALF, D), bf16)]
        + [pltpu.VMEM((1, EXT, HALF), bf16)] * 3
        + [pltpu.VMEM((S + M, HALF), bf16)] * 2
        + [pltpu.VMEM((1, EXT, HALF), bf16), pltpu.SemaphoreType.DMA((2,))],
        6 << 30,
        (n, nm, bank_begin, ctx, x, w_out, gain_f, *blocks1),
        scalars,
        "other_heads",
    )
    ups = [after(w, hid) for w in ups]
    downs = [after(w, hid) for w in downs]
    up_far = moved(ups[1], "y", -1)
    down_far = moved(downs[1], "x", 1)
    up_partners, down_partners = partners(ups), partners(downs)
    memory_other = moved(cut(memory, (1 - h) * HALF, HALF, 2), "m")
    rows = U * F
    nf, hid = nf.reshape(rows, D), hid.reshape(rows, D)
    own = call(
        own_hidden_kernel,
        (4,),
        [
            all_of((rows, D)),
            pl.BlockSpec((D, HALF), lambda j: (0, j)),
            pl.BlockSpec((HALF, D), lambda j: (j, 0)),
        ],
        all_of((rows, D)),
        arrays((rows, D))[0],
        [pltpu.VMEM((rows, D), f32)],
        4 << 30,
        (nf, w_up, w_down),
        None,
        "own_hidden",
    )
    up_far, down_far = after(up_far, own), after(down_far, own)
    ups += [up_far, *up_partners, *partners([up_far])]
    downs += [down_far, *down_partners, *partners([down_far])]
    memory_other, hid = lax.optimization_barrier((memory_other, hid))
    out_own, out_other = call(
        other_hidden_kernel,
        (1,),
        [all_of((rows, D))] * 3 + [ANY] * 16,
        [all_of((U, F, HALF))] * 2,
        arrays((U, F, HALF), (U, F, HALF)),
        [
            pltpu.VMEM((4, D, HALF), bf16),
            pltpu.VMEM((2048, D), bf16),
            pltpu.VMEM((rows, D), f32),
            pltpu.SemaphoreType.DMA((5,)),
        ],
        4 << 30,
        (nf, hid, own, *ups, *downs),
        scalars,
        "other_hidden",
    )
    memory_out = joined(cut(memory, h * HALF, HALF, 2), memory_other, h, 0)
    encoded = joined(out_own, moved(out_other, "m"), h, 0)
    return encoded, memory_out


def solution(mesh):
    in_specs = (
        P(None, "tm", None),
        P(),
        P(None, "tm"),
        P(None, "tm", "mp"),
        P(None, "mp"),
        P(),
        P(None, "mp"),
        P(None, "mp"),
        P(None, "mp"),
        P("mp", None),
        P(),
        P(None, "mp"),
        P("mp", None),
    )
    out_specs = (P(None, "tm", "mp"), P(None, "tm", "mp"))

    return jax.shard_map(
        body, mesh=mesh, in_specs=in_specs, out_specs=out_specs, check_vma=False
    )
```

```python
import jax
import jax.numpy as jnp
from jax import lax
from jax.experimental import pallas as pl
from jax.experimental.pallas import tpu as pltpu
from jax.sharding import PartitionSpec as P


D = 1024
HALF = 512
SEG = 4
LC = 32
RC = 4
M = 32
NX, NZ, NY, NC = 4, 4, 4, 2
TM = NX * NZ * NY * NC
U = 2
F = 256
S = 64
EXT = 320
QB, KB = 160, 256
KF = 192
epsilon = 1e-05
bf16, f32, i32 = jnp.bfloat16, jnp.float32, jnp.int32
AXES = ("tm", "mp")
GRANTS = {
    "pack": 48,
    "front": 48,
    "own_heads": 48,
    "other_heads": 48,
    "own_hidden": 48,
    "other_hidden": 48,
}


def place(x, z, y, c, m):
    return ((((x % NX) * NZ + z) * NY + y % NY) * NC + c % NC) * 2 + m % 2


def route(step):
    dx, dy, dc, dm = step
    return [
        (place(x, z, y, c, m), place(x + dx, z, y + dy, c + dc, m + dm))
        for x in range(NX)
        for z in range(NZ)
        for y in range(NY)
        for c in range(NC)
        for m in range(2)
    ]


STEPS = {
    ("x", 1): (1, 0, 0, 0),
    ("x", -1): (-1, 0, 0, 0),
    ("y", 1): (0, 1, 0, 0),
    ("y", -1): (0, -1, 0, 0),
    ("c", 1): (0, 0, 1, 0),
    ("m", 1): (0, 0, 0, 1),
}


def moved(array, axis, by=1):
    return lax.ppermute(array, AXES, route(STEPS[axis, by]))


def along_frames(array, by):
    pairs = [
        (t * 2 + m, (t + by) * 2 + m) for t in range(TM) for m in range(2) if 0 <= t + by < TM
    ]
    return lax.ppermute(array, AXES, pairs)


def after(value, *earlier):
    return lax.optimization_barrier((value, *earlier))[0]


def both_ways(array, axis, way):
    back = moved(array, axis, way)
    front = moved(array, axis, -way)
    return back, front


def partners(blocks):
    return [moved(b, "c") for b in blocks]


def each_piece(first, way, where, halves):
    x, y, c = where
    near = (0, -way, way, -2 * way)
    far = [(0, 0, 4), (way, 0, 4), (-way, 0, 4)]
    far += [(2, 0, 2), (2, 2, 4)] if halves else [(2, 0, 4)]
    for i, (a2, low, high) in enumerate(far):
        for j in range(low, high):
            a1 = near[j]
            px = (x + (a1 if first == "x" else a2)) & 3
            py = (y + (a2 if first == "x" else a1)) & 3
            for k in range(2):
                pc = c if k == 0 else 1 - c
                yield i + len(far) * k, j - low, px * 8 + py * 2 + pc


def dot(a, b):
    return jnp.dot(a, b, preferred_element_type=f32)


def normed(values, gain):
    center = jnp.sum(values, axis=-1, keepdims=True) * (1.0 / D)
    shifted = values - center
    spread_ = jnp.sum(shifted * shifted, axis=-1, keepdims=True) * (1.0 / D)
    return shifted * lax.rsqrt(spread_ + epsilon) * gain


def gelu(v):
    inner = 0.7978845608028654 * (v + 0.044715 * (v * v * v))
    return 0.5 * v * (1.0 + jnp.tanh(inner))


def pack_kernel(sc, wq, wk, wv, wo, wu, wd, mem, s1, up, down):
    s1[:, :HALF] = wq[...]
    s1[:, HALF : 2 * HALF] = wk[...]
    s1[:, 2 * HALF : 3 * HALF] = wv[...]
    s1[:16, 3 * HALF :] = wo[:, :HALF]
    s1[16:, 3 * HALF :] = wo[:, HALF:]
    up[:, :2048] = wu[...]
    down[...] = wd[...]
    for i in range(4):
        at = slice(2048 + HALF * i, 2048 + HALF * i + HALF)
        up[:, at] = mem[i // 2, 32 * (i % 2) : 32 * (i % 2) + 32, :]


def front_kernel(
    sc, fb, left, right, wf_own, wf_a, wf_b, gain, wq, wk, wv, x_out, n_out, q, k, v, xs, fbs
):
    u = pl.program_id(0)
    h, c = sc[2], sc[5]
    fbs[:LC] = left[0]
    fbs[LC : LC + F] = fb[0]
    fbs[LC + F : LC + F + 16] = right[0]
    fbs[LC + F + 16 :] = jnp.zeros((16, 320), bf16)
    rows = fbs[...]
    pos = sc[3] * F - LC + lax.broadcasted_iota(i32, (EXT, 1), 0)
    valid = pos < sc[u]

    def put(at, width, w):
        part = jnp.where(valid, dot(rows, w[...]), 0.0).astype(bf16)
        xs[:, pl.ds(pl.multiple_of(at, 256), width)] = part

    other = (1 - h) * HALF
    put(h * HALF, HALF, wf_own)
    put(other + c * 256, 256, wf_a)
    put(other + (1 - c) * 256, 256, wf_b)
    x_out[0] = xs[LC : LC + F, :]
    g = gain[...]
    n_out[0, :EXT, :] = normed(xs[...].astype(f32), g).astype(bf16)
    seg = lax.broadcasted_iota(i32, (S, F), 0)
    frame = lax.broadcasted_iota(i32, (S, F), 1)
    pool = jnp.where(frame // SEG == seg, 0.25, 0.0).astype(bf16)
    n_out[0, EXT:, :] = normed(dot(pool, xs[LC : LC + F, :]), g).astype(bf16)
    project(n_out, wq, wk, wv, q, k, v)


def project(n, wq, wk, wv, q, k, v):
    q[0, :F, :] = (dot(n[0, LC : LC + F, :], wq[...]) * 0.125).astype(bf16)
    q[0, F:, :] = (dot(n[0, EXT:, :], wq[...]) * 0.125).astype(bf16)
    k[0] = dot(n[0, :EXT, :], wk[...]).astype(bf16)
    v[0] = dot(n[0, :EXT, :], wv[...]).astype(bf16)


def mask_of(sc, u, b, begins):
    t = sc[3]
    shape = (QB, S)
    r = lax.broadcasted_iota(i32, shape, 0)
    col = lax.broadcasted_iota(i32, shape, 1)
    local = 32 * b + jnp.where(r < 128, r // SEG, r - 128)
    begin = begins[pl.ds(2 * sc[2] + u, 1), :]
    floor = jnp.sum(jnp.where(col == local, begin, 0), axis=-1, keepdims=True)
    r = lax.broadcasted_iota(i32, (QB, 1), 0)
    seg = t * S + 32 * b + jnp.where(r < 128, r // SEG, r - 128)
    k = lax.broadcasted_iota(i32, (QB, KB), 1)
    pos = t * F - LC + 128 * b + k
    bank = t * S - M + 32 * b + k - KF
    low = jnp.maximum(seg * SEG - LC, 0)
    high = jnp.minimum((seg + 1) * SEG + RC, sc[u])
    sees_frame = (k < KF) & (pos >= low) & (pos < high)
    sees_bank = (k >= KF) & (bank >= floor) & (bank <= seg - 1)
    return jnp.where(sees_frame | sees_bank, 0.0, -1e30).astype(f32)


def attend(sc, u, begins, q, k, v, mk, mv, ctx):
    low = lax.broadcasted_iota(i32, (1, 128), 1) < 64

    def block(b, carry):
        mask = mask_of(sc, u, b, begins)
        masks = jnp.concatenate([mask, mask], axis=0)
        at = pl.multiple_of(b * 128, 128)
        few = pl.multiple_of(b * 32, 32)
        fr, sm = pl.ds(at, 128), pl.ds(F + few, 32)
        kr, mr = pl.ds(at, KF), pl.ds(few, 64)
        for p in range(4):
            lanes = slice(128 * p, 128 * p + 128)
            qb = jnp.concatenate([q[0, fr, lanes], q[0, sm, lanes]], axis=0)
            zero = jnp.zeros_like(qb)
            pair = jnp.concatenate([jnp.where(low, qb, zero), jnp.where(low, zero, qb)], axis=0)
            keys = jnp.concatenate([k[0, kr, lanes], mk[mr, lanes]], axis=0)
            values = jnp.concatenate([v[0, kr, lanes], mv[mr, lanes]], axis=0)
            scores = lax.dot_general(
                pair, keys, (((1,), (1,)), ((), ())), preferred_element_type=f32
            )
            weights = jnp.exp(scores + masks)
            total = jnp.sum(weights, axis=-1, keepdims=True)
            shares = (weights * (1.0 / total)).astype(bf16)
            mixed = dot(shares, values)
            part = jnp.where(low, mixed[:QB], mixed[QB:]).astype(bf16)
            ctx[0, fr, lanes] = part[:128]
            ctx[0, sm, lanes] = part[128:]
        return carry

    lax.fori_loop(0, 2, block, 0)


def own_heads_kernel(
    sc, mem_a, mem_b, halo_a, halo_b, begins, gain, wk, wv, q, k, v, ctx, nm, mk, mv, ms
):
    h = sc[2]
    mine = pl.ds(pl.multiple_of(h * HALF, HALF), HALF)
    theirs = pl.ds(pl.multiple_of((1 - h) * HALF, HALF), HALF)
    ms[:M, mine] = halo_a[0]
    ms[M:, mine] = mem_a[0]
    ms[:M, theirs] = halo_b[0]
    ms[M : M + 32, theirs] = mem_b[:, :HALF]
    ms[M + 32 :, theirs] = mem_b[:, HALF:]
    nm[0] = normed(ms[...].astype(f32), gain[...]).astype(bf16)
    mk[...] = dot(nm[0], wk[...]).astype(bf16)
    mv[...] = dot(nm[0], wv[...]).astype(bf16)
    attend(sc, pl.program_id(0), begins, q, k, v, mk, mv, ctx)


def other_heads_kernel(*refs):
    sc, n, nm, begins, ctx_own, x, wo_own, gain = refs[:8]
    parts = refs[8:18]
    hid, nf, memory = refs[18:21]
    wqkv, wo, q, k, v, mk, mv, ctx, sem = refs[21:]
    u = pl.program_id(0)
    where = (sc[4], sc[6], sc[5])

    @pl.when(u == 0)
    def _():
        for r, j, at in each_piece("y", -1, where, True):
            rows = pl.ds(pl.multiple_of(at * 32, 32), 32)
            src = parts[r].at[j, :, : 3 * HALF]
            pltpu.make_async_copy(src, wqkv.at[rows], sem.at[0]).start()
        for r, j, at in each_piece("y", -1, where, True):
            few = pl.ds(pl.multiple_of(at * 16, 16), 16)
            for s in range(2):
                src = parts[r].at[j, 16 * s : 16 * s + 16, 3 * HALF :]
                dst = wo.at[few, HALF * s : HALF * s + HALF]
                pltpu.make_async_copy(src, dst, sem.at[1]).start()

    mine = dot(ctx_own[0], wo_own[...]).astype(bf16).astype(f32)

    @pl.when(u == 0)
    def _():
        pltpu.make_async_copy(wqkv, wqkv, sem.at[0]).wait()
        pltpu.make_async_copy(wo, wo, sem.at[1]).wait()

    wk, wv = wqkv.at[:, HALF : 2 * HALF], wqkv.at[:, 2 * HALF :]
    project(n, wqkv.at[:, :HALF], wk, wv, q, k, v)
    mk[...] = dot(nm[0], wk[...]).astype(bf16)
    mv[...] = dot(nm[0], wv[...]).astype(bf16)
    attend(sc, u, begins, q, k, v, mk, mv, ctx)
    theirs = dot(ctx[0], wo[...]).astype(bf16).astype(f32)
    both = mine + theirs
    seg = sc[3] * S + lax.broadcasted_iota(i32, (S, 1), 0)
    memory[0] = jnp.where(seg * SEG < sc[u], both[F:], 0.0).astype(bf16)
    residual = (x[0].astype(f32) + both[:F]).astype(bf16)
    hid[...] = residual
    nf[...] = normed(residual.astype(f32), gain[...]).astype(bf16)


def own_hidden_kernel(nf, wu, wd, out, acc):
    j = pl.program_id(0)
    hidden = gelu(dot(nf[...], wu[...])).astype(bf16)
    part = dot(hidden, wd[...])

    @pl.when(j == 0)
    def _():
        acc[...] = part

    @pl.when(j > 0)
    def _():
        acc[...] += part

    @pl.when(j == pl.num_programs(0) - 1)
    def _():
        out[...] = acc[...].astype(bf16)


def other_hidden_kernel(*refs):
    sc, nf, hid, own = refs[:4]
    ups, downs = refs[4:12], refs[12:20]
    out_own, out_other = refs[20:22]
    wu, wd, acc, sem = refs[22:]
    where = (sc[4], sc[6], sc[5])

    def fetch_up(i):
        for r, j, at in each_piece("x", 1, where, False):
            rows = pl.ds(pl.multiple_of(at * 32, 32), 32)
            src = ups[r].at[j, :, HALF * i : HALF * i + HALF]
            pltpu.make_async_copy(src, wu.at[i, rows], sem.at[i]).start()

    fetch_up(0)
    for r, j, at in each_piece("y", -1, where, False):
        rows = pl.ds(pl.multiple_of(at * 64, 64), 64)
        pltpu.make_async_copy(downs[r].at[j], wd.at[rows], sem.at[4]).start()
    for i in range(1, 4):
        fetch_up(i)

    def step(i, carry):
        pltpu.make_async_copy(wu.at[i], wu.at[i], sem.at[i]).wait()
        hidden = gelu(dot(nf[...], wu[i])).astype(bf16)

        @pl.when(i == 0)
        def _():
            pltpu.make_async_copy(wd, wd, sem.at[4]).wait()
            acc[...] = jnp.zeros_like(acc)

        acc[...] += dot(hidden, wd[pl.ds(pl.multiple_of(i * HALF, HALF), HALF)])
        return carry

    lax.fori_loop(0, 4, step, 0)
    h = sc[2]
    row = lax.broadcasted_iota(i32, (F, 1), 0)
    for u in range(U):
        valid = sc[3] * F + row < sc[u]
        at = slice(F * u, F * u + F)
        for out, start in ((out_own, h * HALF), (out_other, (1 - h) * HALF)):
            cols = pl.ds(pl.multiple_of(start, HALF), HALF)
            feed = own[at, cols].astype(f32) + acc[at, cols].astype(bf16).astype(f32)
            whole = hid[at, cols].astype(f32) + feed
            out[u] = jnp.where(valid, whole, 0.0).astype(bf16)


def one(shape):
    return pl.BlockSpec((1,) + shape, lambda u, *_: (u,) + (0,) * len(shape))


def all_of(shape):
    return pl.BlockSpec(shape, lambda *_: (0,) * len(shape))


ANY = pl.BlockSpec(memory_space=pl.ANY)


def arrays(*shapes):
    return [jax.ShapeDtypeStruct(s, bf16) for s in shapes]


def kept(*shapes):
    return [pltpu.HBM(s, bf16) for s in shapes]


def stored(array):
    return pltpu.with_memory_space_constraint(array, pltpu.HBM)


def call(kernel, grid, ins, outs, out_shape, scratch, flops, args, scalars=None, name=None):
    spec = pltpu.PrefetchScalarGridSpec(
        num_scalar_prefetch=0 if scalars is None else 1,
        grid=grid,
        in_specs=ins,
        out_specs=outs,
        scratch_shapes=scratch,
    )
    given = list(args) if scalars is None else [scalars, *args]
    return pl.pallas_call(
        kernel,
        grid_spec=spec,
        out_shape=out_shape,
        compiler_params=pltpu.CompilerParams(
            dimension_semantics=("arbitrary",) * len(grid), vmem_limit_bytes=GRANTS[name] << 20
        ),
        cost_estimate=pl.CostEstimate(
            flops=flops, bytes_accessed=8 << 20, transcendentals=1 << 20
        ),
    )(*given)


def cut(array, at, size, dim):
    return lax.dynamic_slice_in_dim(array, at, size, dim)


def joined(own, other, h, dim):
    return jnp.where(
        h == 0,
        jnp.concatenate([own, other], axis=dim),
        jnp.concatenate([other, own], axis=dim),
    )


def body(
    filterbank,
    lengths,
    bank_begin,
    memory_in,
    w_front,
    gain_attn,
    w_query,
    w_key,
    w_value,
    w_out,
    gain_ffn,
    w_up,
    w_down,
):
    t, h = lax.axis_index("tm"), lax.axis_index("mp")
    x_at, y_at, c_at = t // (NZ * NY * NC), (t // NC) % NY, t % NC
    piece = x_at * 8 + y_at * 2 + c_at
    lens = cut(lengths, 2 * h, 2, 0)
    scalars = jnp.concatenate([lens, jnp.stack([h, t, x_at, c_at, y_at, piece]).astype(i32)])

    gain_a, gain_f = gain_attn.reshape(1, D), gain_ffn.reshape(1, D)

    wf_cut = cut(w_front, c_at * 256, 256, 1)
    wf_a = moved(wf_cut, "m")
    wf_b = moved(wf_a, "c")

    def piece_of(rows, width):
        return pl.BlockSpec((rows, width), lambda i, sc: (sc[7], 0))

    weights = [stored(w) for w in (w_query, w_key, w_value, w_out, w_up, w_down)]
    w_query, w_key, w_value, w_out, w_up, w_down = weights
    memory_all = stored(memory_in)
    s1, up, down = call(
        pack_kernel,
        (1,),
        [piece_of(32, HALF)] * 3 + [piece_of(16, D), piece_of(32, 2048), piece_of(64, D)]
        + [pl.BlockSpec((2, S, HALF), lambda i, sc: (1 - sc[2], 0, 0))],
        [all_of((32, 2048)), all_of((32, 4096)), all_of((64, D))],
        arrays((32, 2048), (32, 4096), (64, D)),
        [],
        1 << 20,
        (w_query, w_key, w_value, w_out, w_up, w_down, memory_all),
        after(scalars, wf_cut),
        "pack",
    )
    filterbank = after(filterbank, up)
    s1 = moved(s1, "m")
    up = moved(up, "m")
    down = moved(down, "m")
    back, front = both_ways(s1, "y", -1)
    filled1 = jnp.stack([s1, back, front, moved(back, "y", -1)])
    back1, front1 = both_ways(filled1, "x", 1)

    fb = filterbank.reshape(4, F, 320)
    mine = cut(fb, 2 * h, 2, 0)
    left = along_frames(mine[:, F - LC :], 1)
    right = along_frames(mine[:, :16], -1)
    halo_own = along_frames(cut(memory_in, 2 * h, 2, 0)[:, S - M :], 1)

    x, n, q, kk, v = call(
        front_kernel,
        (U,),
        [pl.BlockSpec((1, F, 320), lambda u, sc: (2 * sc[2] + u, 0, 0))]
        + [one((LC, 320)), one((16, 320))]
        + [all_of((320, HALF)), all_of((320, 256)), all_of((320, 256))]
        + [all_of((1, D))]
        + [all_of((D, HALF))] * 3,
        [one((F, D)), one((EXT + S, D))] + [one((EXT, HALF))] * 3,
        kept((U, F, D), (U, EXT + S, D), *[(U, EXT, HALF)] * 3),
        [pltpu.VMEM((EXT, D), bf16), pltpu.VMEM((EXT, 320), bf16)],
        2 * 640 * 1024 * 1536,
        (fb, left, right, w_front, wf_a, wf_b, gain_a, w_query, w_key, w_value),
        scalars,
        "front",
    )
    up, down = after(up, x), after(down, x)
    mem_other, up = up, up[:, :2048]
    late = [mem_other[:, at : at + HALF] for at in (2560, 3584)]
    halo_other = along_frames(jnp.stack(late), 1)
    up_back, up_front = both_ways(up, "x", 1)
    down_back, down_front = both_ways(down, "y", -1)
    ctx, nm = call(
        own_heads_kernel,
        (U,),
        [pl.BlockSpec((1, S, HALF), lambda u, sc: (2 * sc[2] + u, 0, 0))]
        + [pl.BlockSpec((32, D), lambda u, sc: (0, 2 + u))]
        + [one((M, HALF))] * 2
        + [all_of((4, S)), all_of((1, D)), all_of((D, HALF)), all_of((D, HALF))]
        + [one((EXT, HALF))] * 3,
        [one((EXT, HALF)), one((S + M, D))],
        kept((U, EXT, HALF), (U, S + M, D)),
        [pltpu.VMEM((S + M, HALF), bf16)] * 2 + [pltpu.VMEM((S + M, D), bf16)],
        2 << 30,
        (memory_all, mem_other, halo_own, halo_other, bank_begin, gain_a, w_key, w_value, *map(stored, (q, kk, v))),
        scalars,
        "own_heads",
    )
    up_back, down_back = after(up_back, ctx), after(down_back, ctx)
    ups = jnp.stack([up, up_back, up_front, moved(up_back, "x", 1)])
    downs = jnp.stack([down, down_back, down_front, moved(down_back, "y", -1)])
    ups = [ups, *both_ways(ups, "y", -1)]
    downs = [downs, *both_ways(downs, "x", 1)]
    back1, front1, filled1 = after(back1, ctx), after(front1, ctx), after(filled1, ctx)
    blocks1 = [filled1, back1, front1]
    blocks1 += [moved(back1[:2], "x", 1), moved(front1[2:], "x", -1)]
    blocks1 += partners(blocks1)
    hid, nf, memory = call(
        other_heads_kernel,
        (U,),
        [one((EXT + S, D)), one((S + M, D)), all_of((4, S)), one((EXT, HALF)), one((F, D))]
        + [all_of((HALF, D)), all_of((1, D))]
        + [ANY] * 10,
        [pl.BlockSpec((F, D), lambda u, *_: (u, 0))] * 2 + [one((S, D))],
        kept((U * F, D), (U * F, D)) + arrays((U, S, D)),
        [pltpu.VMEM((D, 3 * HALF), bf16), pltpu.VMEM((HALF, D), bf16)]
        + [pltpu.VMEM((1, EXT, HALF), bf16)] * 3
        + [pltpu.VMEM((S + M, HALF), bf16)] * 2
        + [pltpu.VMEM((1, EXT, HALF), bf16), pltpu.SemaphoreType.DMA((2,))],
        6 << 30,
        (stored(n), stored(nm), bank_begin, stored(ctx), stored(x), w_out, gain_f, *blocks1),
        scalars,
        "other_heads",
    )
    ups = [after(w, hid) for w in ups]
    downs = [after(w, hid) for w in downs]
    up_far = moved(ups[1], "y", -1)
    down_far = moved(downs[1], "x", 1)
    up_partners, down_partners = partners(ups), partners(downs)
    memory_other = moved(cut(memory, (1 - h) * HALF, HALF, 2), "m")
    rows = U * F
    own = call(
        own_hidden_kernel,
        (4,),
        [
            all_of((rows, D)),
            pl.BlockSpec((D, HALF), lambda j: (0, j)),
            pl.BlockSpec((HALF, D), lambda j: (j, 0)),
        ],
        all_of((rows, D)),
        kept((rows, D))[0],
        [pltpu.VMEM((rows, D), f32)],
        4 << 30,
        (stored(nf), w_up, w_down),
        None,
        "own_hidden",
    )
    up_far, down_far = after(up_far, own), after(down_far, own)
    ups += [up_far, *up_partners, *partners([up_far])]
    downs += [down_far, *down_partners, *partners([down_far])]
    memory_other, hid = lax.optimization_barrier((memory_other, hid))
    out_own, out_other = call(
        other_hidden_kernel,
        (1,),
        [all_of((rows, D))] * 3 + [ANY] * 16,
        [all_of((U, F, HALF))] * 2,
        arrays((U, F, HALF), (U, F, HALF)),
        [
            pltpu.VMEM((4, D, HALF), bf16),
            pltpu.VMEM((2048, D), bf16),
            pltpu.VMEM((rows, D), f32),
            pltpu.SemaphoreType.DMA((5,)),
        ],
        4 << 30,
        (stored(nf), stored(hid), stored(own), *ups, *downs),
        scalars,
        "other_hidden",
    )
    memory_out = joined(cut(memory, h * HALF, HALF, 2), memory_other, h, 0)
    encoded = joined(out_own, moved(out_other, "m"), h, 0)
    return encoded, memory_out


def solution(mesh):
    in_specs = (
        P(None, "tm", None),
        P(),
        P(None, "tm"),
        P(None, "tm", "mp"),
        P(None, "mp"),
        P(),
        P(None, "mp"),
        P(None, "mp"),
        P(None, "mp"),
        P("mp", None),
        P(),
        P(None, "mp"),
        P("mp", None),
    )
    out_specs = (P(None, "tm", "mp"), P(None, "tm", "mp"))

    return jax.shard_map(
        body, mesh=mesh, in_specs=in_specs, out_specs=out_specs, check_vma=False
    )
```

```python
import jax
import jax.numpy as jnp
from jax import lax
from jax.experimental import pallas as pl
from jax.experimental.pallas import tpu as pltpu
from jax.sharding import PartitionSpec as P


D = 1024
HALF = 512
SEG = 4
LC = 32
RC = 4
M = 32
NX, NZ, NY, NC = 4, 4, 4, 2
TM = NX * NZ * NY * NC
U = 2
F = 256
S = 64
EXT = 320
QB, KB = 160, 256
KF = 192
epsilon = 1e-05
bf16, f32, i32 = jnp.bfloat16, jnp.float32, jnp.int32
AXES = ("tm", "mp")
GRANTS = {
    "pack": 48,
    "front": 48,
    "own_heads": 48,
    "other_heads": 48,
    "own_hidden": 48,
    "other_hidden": 48,
}


def place(x, z, y, c, m):
    return ((((x % NX) * NZ + z) * NY + y % NY) * NC + c % NC) * 2 + m % 2


def route(step):
    dx, dy, dc, dm = step
    return [
        (place(x, z, y, c, m), place(x + dx, z, y + dy, c + dc, m + dm))
        for x in range(NX)
        for z in range(NZ)
        for y in range(NY)
        for c in range(NC)
        for m in range(2)
    ]


STEPS = {
    ("x", 1): (1, 0, 0, 0),
    ("x", -1): (-1, 0, 0, 0),
    ("y", 1): (0, 1, 0, 0),
    ("y", -1): (0, -1, 0, 0),
    ("c", 1): (0, 0, 1, 0),
    ("m", 1): (0, 0, 0, 1),
}


def moved(array, axis, by=1):
    return lax.ppermute(array, AXES, route(STEPS[axis, by]))


def along_frames(array, by):
    pairs = [
        (t * 2 + m, (t + by) * 2 + m) for t in range(TM) for m in range(2) if 0 <= t + by < TM
    ]
    return lax.ppermute(array, AXES, pairs)


def after(value, *earlier):
    return lax.optimization_barrier((value, *earlier))[0]


def both_ways(array, axis, way):
    back = moved(array, axis, way)
    front = moved(array, axis, -way)
    return back, front


def partners(blocks):
    return [moved(b, "c") for b in blocks]


def each_piece(first, way, where, halves, act):
    x, y, c = where
    far = [(0, 0, 4), (way, 0, 4), (-way, 0, 4)]
    far += [(2, 0, 2), (2, 2, 4)] if halves else [(2, 0, 4)]
    for i, (a2, low, high) in enumerate(far):

        def step(j, carry):
            a1 = jnp.where(j == 0, 0, jnp.where(j == 1, -way, jnp.where(j == 2, way, 2)))
            px = (x + (a1 if first == "x" else a2)) & 3
            py = (y + (a2 if first == "x" else a1)) & 3
            for k in range(2):
                pc = c if k == 0 else 1 - c
                act(i + len(far) * k, j - low, px * 8 + py * 2 + pc)
            return carry

        lax.fori_loop(low, high, step, 0)


def dot(a, b):
    return jnp.dot(a, b, preferred_element_type=f32)


def normed(values, gain):
    center = jnp.sum(values, axis=-1, keepdims=True) * (1.0 / D)
    shifted = values - center
    spread_ = jnp.sum(shifted * shifted, axis=-1, keepdims=True) * (1.0 / D)
    return shifted * lax.rsqrt(spread_ + epsilon) * gain


def gelu(v):
    inner = 0.7978845608028654 * (v + 0.044715 * (v * v * v))
    return 0.5 * v * (1.0 + jnp.tanh(inner))


def pack_kernel(sc, wq, wk, wv, wo, wu, wd, mem, s1, up, down):
    s1[:, :HALF] = wq[...]
    s1[:, HALF : 2 * HALF] = wk[...]
    s1[:, 2 * HALF : 3 * HALF] = wv[...]
    s1[:16, 3 * HALF :] = wo[:, :HALF]
    s1[16:, 3 * HALF :] = wo[:, HALF:]
    up[:, :2048] = wu[...]
    down[...] = wd[...]
    for i in range(4):
        at = slice(2048 + HALF * i, 2048 + HALF * i + HALF)
        up[:, at] = mem[i // 2, 32 * (i % 2) : 32 * (i % 2) + 32, :]


def front_kernel(
    sc, fb, left, right, wf_own, wf_a, wf_b, gain, wq, wk, wv, x_out, n_out, q, k, v, xs, fbs
):
    u = pl.program_id(0)
    h, c = sc[2], sc[5]
    fbs[:LC] = left[0]
    fbs[LC : LC + F] = fb[0]
    fbs[LC + F : LC + F + 16] = right[0]
    fbs[LC + F + 16 :] = jnp.zeros((16, 320), bf16)
    rows = fbs[...]
    pos = sc[3] * F - LC + lax.broadcasted_iota(i32, (EXT, 1), 0)
    valid = pos < sc[u]

    def put(at, width, w):
        part = jnp.where(valid, dot(rows, w[...]), 0.0).astype(bf16)
        xs[:, pl.ds(pl.multiple_of(at, 256), width)] = part

    other = (1 - h) * HALF
    put(h * HALF, HALF, wf_own)
    put(other + c * 256, 256, wf_a)
    put(other + (1 - c) * 256, 256, wf_b)
    x_out[0] = xs[LC : LC + F, :]
    g = gain[...]
    n_out[0, :EXT, :] = normed(xs[...].astype(f32), g).astype(bf16)
    seg = lax.broadcasted_iota(i32, (S, F), 0)
    frame = lax.broadcasted_iota(i32, (S, F), 1)
    pool = jnp.where(frame // SEG == seg, 0.25, 0.0).astype(bf16)
    n_out[0, EXT:, :] = normed(dot(pool, xs[LC : LC + F, :]), g).astype(bf16)
    project(n_out, wq, wk, wv, q, k, v)


def project(n, wq, wk, wv, q, k, v):
    q[0, :F, :] = (dot(n[0, LC : LC + F, :], wq[...]) * 0.125).astype(bf16)
    q[0, F:, :] = (dot(n[0, EXT:, :], wq[...]) * 0.125).astype(bf16)
    k[0] = dot(n[0, :EXT, :], wk[...]).astype(bf16)
    v[0] = dot(n[0, :EXT, :], wv[...]).astype(bf16)


def mask_of(sc, u, b, begins):
    t = sc[3]
    shape = (QB, S)
    r = lax.broadcasted_iota(i32, shape, 0)
    col = lax.broadcasted_iota(i32, shape, 1)
    local = 32 * b + jnp.where(r < 128, r // SEG, r - 128)
    begin = begins[pl.ds(2 * sc[2] + u, 1), :]
    floor = jnp.sum(jnp.where(col == local, begin, 0), axis=-1, keepdims=True)
    r = lax.broadcasted_iota(i32, (QB, 1), 0)
    seg = t * S + 32 * b + jnp.where(r < 128, r // SEG, r - 128)
    k = lax.broadcasted_iota(i32, (QB, KB), 1)
    pos = t * F - LC + 128 * b + k
    bank = t * S - M + 32 * b + k - KF
    low = jnp.maximum(seg * SEG - LC, 0)
    high = jnp.minimum((seg + 1) * SEG + RC, sc[u])
    sees_frame = (k < KF) & (pos >= low) & (pos < high)
    sees_bank = (k >= KF) & (bank >= floor) & (bank <= seg - 1)
    return jnp.where(sees_frame | sees_bank, 0.0, -1e30).astype(f32)


def attend(sc, u, begins, q, k, v, mk, mv, ctx):
    low = lax.broadcasted_iota(i32, (1, 128), 1) < 64

    def block(b, carry):
        mask = mask_of(sc, u, b, begins)
        masks = jnp.concatenate([mask, mask], axis=0)
        at = pl.multiple_of(b * 128, 128)
        few = pl.multiple_of(b * 32, 32)
        fr, sm = pl.ds(at, 128), pl.ds(F + few, 32)
        kr, mr = pl.ds(at, KF), pl.ds(few, 64)
        for p in range(4):
            lanes = slice(128 * p, 128 * p + 128)
            qb = jnp.concatenate([q[0, fr, lanes], q[0, sm, lanes]], axis=0)
            zero = jnp.zeros_like(qb)
            pair = jnp.concatenate([jnp.where(low, qb, zero), jnp.where(low, zero, qb)], axis=0)
            keys = jnp.concatenate([k[0, kr, lanes], mk[mr, lanes]], axis=0)
            values = jnp.concatenate([v[0, kr, lanes], mv[mr, lanes]], axis=0)
            scores = lax.dot_general(
                pair, keys, (((1,), (1,)), ((), ())), preferred_element_type=f32
            )
            weights = jnp.exp(scores + masks)
            total = jnp.sum(weights, axis=-1, keepdims=True)
            shares = (weights * (1.0 / total)).astype(bf16)
            mixed = dot(shares, values)
            part = jnp.where(low, mixed[:QB], mixed[QB:]).astype(bf16)
            ctx[0, fr, lanes] = part[:128]
            ctx[0, sm, lanes] = part[128:]
        return carry

    lax.fori_loop(0, 2, block, 0)


def own_heads_kernel(
    sc, mem_a, mem_b, halo_a, halo_b, begins, gain, wk, wv, q, k, v, ctx, nm, mk, mv, ms
):
    h = sc[2]
    mine = pl.ds(pl.multiple_of(h * HALF, HALF), HALF)
    theirs = pl.ds(pl.multiple_of((1 - h) * HALF, HALF), HALF)
    ms[:M, mine] = halo_a[0]
    ms[M:, mine] = mem_a[0]
    ms[:M, theirs] = halo_b[0]
    ms[M : M + 32, theirs] = mem_b[:, :HALF]
    ms[M + 32 :, theirs] = mem_b[:, HALF:]
    nm[0] = normed(ms[...].astype(f32), gain[...]).astype(bf16)
    mk[...] = dot(nm[0], wk[...]).astype(bf16)
    mv[...] = dot(nm[0], wv[...]).astype(bf16)
    attend(sc, pl.program_id(0), begins, q, k, v, mk, mv, ctx)


def other_heads_kernel(*refs):
    sc, n, nm, begins, ctx_own, x, wo_own, gain = refs[:8]
    parts = refs[8:18]
    hid, nf, memory = refs[18:21]
    wqkv, wo, q, k, v, mk, mv, ctx, sem = refs[21:]
    u = pl.program_id(0)
    where = (sc[4], sc[6], sc[5])

    @pl.when(u == 0)
    def _():
        def fetch(r, j, at):
            rows = pl.ds(pl.multiple_of(at * 32, 32), 32)
            src = parts[r].at[j, :, : 3 * HALF]
            pltpu.make_async_copy(src, wqkv.at[rows], sem.at[0]).start()
            few = pl.ds(pl.multiple_of(at * 16, 16), 16)
            for s in range(2):
                src = parts[r].at[j, 16 * s : 16 * s + 16, 3 * HALF :]
                dst = wo.at[few, HALF * s : HALF * s + HALF]
                pltpu.make_async_copy(src, dst, sem.at[1]).start()

        each_piece("y", -1, where, True, fetch)

    mine = dot(ctx_own[0], wo_own[...]).astype(bf16).astype(f32)

    @pl.when(u == 0)
    def _():
        pltpu.make_async_copy(wqkv, wqkv, sem.at[0]).wait()
        pltpu.make_async_copy(wo, wo, sem.at[1]).wait()

    wk, wv = wqkv.at[:, HALF : 2 * HALF], wqkv.at[:, 2 * HALF :]
    project(n, wqkv.at[:, :HALF], wk, wv, q, k, v)
    mk[...] = dot(nm[0], wk[...]).astype(bf16)
    mv[...] = dot(nm[0], wv[...]).astype(bf16)
    attend(sc, u, begins, q, k, v, mk, mv, ctx)
    theirs = dot(ctx[0], wo[...]).astype(bf16).astype(f32)
    both = mine + theirs
    seg = sc[3] * S + lax.broadcasted_iota(i32, (S, 1), 0)
    memory[0] = jnp.where(seg * SEG < sc[u], both[F:], 0.0).astype(bf16)
    residual = (x[0].astype(f32) + both[:F]).astype(bf16)
    hid[...] = residual
    nf[...] = normed(residual.astype(f32), gain[...]).astype(bf16)


def own_hidden_kernel(nf, wu, wd, out, acc):
    j = pl.program_id(0)

    def some(r, carry):
        rows = pl.ds(pl.multiple_of(r * F, F), F)
        hidden = gelu(dot(nf[rows], wu[...])).astype(bf16)
        part = dot(hidden, wd[...])
        acc[rows] = jnp.where(j == 0, part, acc[rows] + part)
        return carry

    lax.fori_loop(0, U, some, 0)

    @pl.when(j == pl.num_programs(0) - 1)
    def _():
        out[...] = acc[...].astype(bf16)


def other_hidden_kernel(*refs):
    sc, nf, hid, own = refs[:4]
    ups, downs = refs[4:12], refs[12:20]
    out_own, out_other = refs[20:22]
    wu, wd, acc, sem = refs[22:]
    where = (sc[4], sc[6], sc[5])

    def fetch_up(i):
        def fetch(r, j, at):
            rows = pl.ds(pl.multiple_of(at * 32, 32), 32)
            cols = pl.ds(pl.multiple_of(i * HALF, HALF), HALF)
            pltpu.make_async_copy(ups[r].at[j, :, cols], wu.at[i, rows], sem.at[i]).start()

        each_piece("x", 1, where, False, fetch)

    def fetch_down(r, j, at):
        rows = pl.ds(pl.multiple_of(at * 64, 64), 64)
        pltpu.make_async_copy(downs[r].at[j], wd.at[rows], sem.at[4]).start()

    fetch_up(0)
    each_piece("y", -1, where, False, fetch_down)

    def fetch_rest(i, carry):
        fetch_up(i)
        return carry

    lax.fori_loop(1, 4, fetch_rest, 0)

    def step(i, carry):
        pltpu.make_async_copy(wu.at[i], wu.at[i], sem.at[i]).wait()

        @pl.when(i == 0)
        def _():
            pltpu.make_async_copy(wd, wd, sem.at[4]).wait()
            acc[...] = jnp.zeros_like(acc)

        def some(r, carry):
            rows = pl.ds(pl.multiple_of(r * F, F), F)
            hidden = gelu(dot(nf[rows], wu[i])).astype(bf16)
            acc[rows] += dot(hidden, wd[pl.ds(pl.multiple_of(i * HALF, HALF), HALF)])
            return carry

        return lax.fori_loop(0, U, some, carry)

    lax.fori_loop(0, 4, step, 0)
    h = sc[2]
    row = lax.broadcasted_iota(i32, (F, 1), 0)
    for u in range(U):
        valid = sc[3] * F + row < sc[u]
        at = slice(F * u, F * u + F)
        for out, start in ((out_own, h * HALF), (out_other, (1 - h) * HALF)):
            cols = pl.ds(pl.multiple_of(start, HALF), HALF)
            feed = own[at, cols].astype(f32) + acc[at, cols].astype(bf16).astype(f32)
            whole = hid[at, cols].astype(f32) + feed
            out[u] = jnp.where(valid, whole, 0.0).astype(bf16)


def one(shape):
    return pl.BlockSpec((1,) + shape, lambda u, *_: (u,) + (0,) * len(shape))


def all_of(shape):
    return pl.BlockSpec(shape, lambda *_: (0,) * len(shape))


ANY = pl.BlockSpec(memory_space=pl.ANY)


def arrays(*shapes):
    return [jax.ShapeDtypeStruct(s, bf16) for s in shapes]


def kept(*shapes):
    return [pltpu.HBM(s, bf16) for s in shapes]


def stored(array):
    return pltpu.with_memory_space_constraint(array, pltpu.HBM)


def call(kernel, grid, ins, outs, out_shape, scratch, flops, args, scalars=None, name=None):
    spec = pltpu.PrefetchScalarGridSpec(
        num_scalar_prefetch=0 if scalars is None else 1,
        grid=grid,
        in_specs=ins,
        out_specs=outs,
        scratch_shapes=scratch,
    )
    given = list(args) if scalars is None else [scalars, *args]
    return pl.pallas_call(
        kernel,
        grid_spec=spec,
        out_shape=out_shape,
        compiler_params=pltpu.CompilerParams(
            dimension_semantics=("arbitrary",) * len(grid), vmem_limit_bytes=GRANTS[name] << 20
        ),
        cost_estimate=pl.CostEstimate(
            flops=flops, bytes_accessed=8 << 20, transcendentals=1 << 20
        ),
    )(*given)


def cut(array, at, size, dim):
    return lax.dynamic_slice_in_dim(array, at, size, dim)


def joined(own, other, h, dim):
    return jnp.where(
        h == 0,
        jnp.concatenate([own, other], axis=dim),
        jnp.concatenate([other, own], axis=dim),
    )


def body(
    filterbank,
    lengths,
    bank_begin,
    memory_in,
    w_front,
    gain_attn,
    w_query,
    w_key,
    w_value,
    w_out,
    gain_ffn,
    w_up,
    w_down,
):
    t, h = lax.axis_index("tm"), lax.axis_index("mp")
    x_at, y_at, c_at = t // (NZ * NY * NC), (t // NC) % NY, t % NC
    piece = x_at * 8 + y_at * 2 + c_at
    lens = cut(lengths, 2 * h, 2, 0)
    scalars = jnp.concatenate([lens, jnp.stack([h, t, x_at, c_at, y_at, piece]).astype(i32)])

    gain_a, gain_f = gain_attn.reshape(1, D), gain_ffn.reshape(1, D)

    wf_cut = cut(w_front, c_at * 256, 256, 1)
    wf_a = moved(wf_cut, "m")
    wf_b = moved(wf_a, "c")

    def piece_of(rows, width):
        return pl.BlockSpec((rows, width), lambda i, sc: (sc[7], 0))

    weights = [stored(w) for w in (w_query, w_key, w_value, w_out, w_up, w_down)]
    w_query, w_key, w_value, w_out, w_up, w_down = weights
    memory_all = stored(memory_in)
    s1, up, down = call(
        pack_kernel,
        (1,),
        [piece_of(32, HALF)] * 3 + [piece_of(16, D), piece_of(32, 2048), piece_of(64, D)]
        + [pl.BlockSpec((2, S, HALF), lambda i, sc: (1 - sc[2], 0, 0))],
        [all_of((32, 2048)), all_of((32, 4096)), all_of((64, D))],
        arrays((32, 2048), (32, 4096), (64, D)),
        [],
        1 << 20,
        (w_query, w_key, w_value, w_out, w_up, w_down, memory_all),
        after(scalars, wf_cut),
        "pack",
    )
    filterbank = after(filterbank, up)
    s1 = moved(s1, "m")
    up = moved(up, "m")
    down = moved(down, "m")
    back, front = both_ways(s1, "y", -1)
    third = moved(back, "y", -1)
    filled1 = jnp.stack([s1, back, front, third])
    back1, front1 = both_ways(filled1, "x", 1)

    fb = filterbank.reshape(4, F, 320)
    mine = cut(fb, 2 * h, 2, 0)
    left = along_frames(mine[:, F - LC :], 1)
    right = along_frames(mine[:, :16], -1)
    halo_own = along_frames(cut(memory_in, 2 * h, 2, 0)[:, S - M :], 1)

    x, n, q, kk, v = call(
        front_kernel,
        (U,),
        [pl.BlockSpec((1, F, 320), lambda u, sc: (2 * sc[2] + u, 0, 0))]
        + [one((LC, 320)), one((16, 320))]
        + [all_of((320, HALF)), all_of((320, 256)), all_of((320, 256))]
        + [all_of((1, D))]
        + [all_of((D, HALF))] * 3,
        [one((F, D)), one((EXT + S, D))] + [one((EXT, HALF))] * 3,
        kept((U, F, D), (U, EXT + S, D), *[(U, EXT, HALF)] * 3),
        [pltpu.VMEM((EXT, D), bf16), pltpu.VMEM((EXT, 320), bf16)],
        2 * 640 * 1024 * 1536,
        (fb, left, right, w_front, wf_a, wf_b, gain_a, w_query, w_key, w_value),
        scalars,
        "front",
    )
    mem_other, up = up, up[:, :2048]
    late = [mem_other[:, at : at + HALF] for at in (2560, 3584)]
    halo_other = along_frames(jnp.stack(late), 1)
    up_back, up_front = both_ways(up, "x", 1)
    down_back, down_front = both_ways(down, "y", -1)
    ctx, nm = call(
        own_heads_kernel,
        (U,),
        [pl.BlockSpec((1, S, HALF), lambda u, sc: (2 * sc[2] + u, 0, 0))]
        + [pl.BlockSpec((32, D), lambda u, sc: (0, 2 + u))]
        + [one((M, HALF))] * 2
        + [all_of((4, S)), all_of((1, D)), all_of((D, HALF)), all_of((D, HALF))]
        + [one((EXT, HALF))] * 3,
        [one((EXT, HALF)), one((S + M, D))],
        kept((U, EXT, HALF), (U, S + M, D)),
        [pltpu.VMEM((S + M, HALF), bf16)] * 2 + [pltpu.VMEM((S + M, D), bf16)],
        2 << 30,
        (memory_all, mem_other, halo_own, halo_other, bank_begin, gain_a, w_key, w_value, *map(stored, (q, kk, v))),
        scalars,
        "own_heads",
    )
    up_back, down_back = after(up_back, ctx), after(down_back, ctx)
    ups = jnp.stack([up, up_back, up_front, moved(up_back, "x", 1)])
    downs = jnp.stack([down, down_back, down_front, moved(down_back, "y", -1)])
    ups = [ups, *both_ways(ups, "y", -1)]
    downs = [downs, *both_ways(downs, "x", 1)]
    back1, front1, filled1 = after(back1, ctx), after(front1, ctx), after(filled1, ctx)
    blocks1 = [filled1, back1, front1]
    blocks1 += [moved(back1[:2], "x", 1), moved(front1[2:], "x", -1)]
    blocks1 += partners(blocks1)
    hid, nf, memory = call(
        other_heads_kernel,
        (U,),
        [one((EXT + S, D)), one((S + M, D)), all_of((4, S)), one((EXT, HALF)), one((F, D))]
        + [all_of((HALF, D)), all_of((1, D))]
        + [ANY] * 10,
        [pl.BlockSpec((F, D), lambda u, *_: (u, 0))] * 2 + [one((S, D))],
        kept((U * F, D), (U * F, D)) + arrays((U, S, D)),
        [pltpu.VMEM((D, 3 * HALF), bf16), pltpu.VMEM((HALF, D), bf16)]
        + [pltpu.VMEM((1, EXT, HALF), bf16)] * 3
        + [pltpu.VMEM((S + M, HALF), bf16)] * 2
        + [pltpu.VMEM((1, EXT, HALF), bf16), pltpu.SemaphoreType.DMA((2,))],
        6 << 30,
        (stored(n), stored(nm), bank_begin, stored(ctx), stored(x), w_out, gain_f, *blocks1),
        scalars,
        "other_heads",
    )
    ups = [after(w, hid) for w in ups]
    downs = [after(w, hid) for w in downs]
    up_far = moved(ups[1], "y", -1)
    down_far = moved(downs[1], "x", 1)
    up_partners, down_partners = partners(ups), partners(downs)
    memory_other = moved(cut(memory, (1 - h) * HALF, HALF, 2), "m")
    rows = U * F
    own = call(
        own_hidden_kernel,
        (4,),
        [
            all_of((rows, D)),
            pl.BlockSpec((D, HALF), lambda j: (0, j)),
            pl.BlockSpec((HALF, D), lambda j: (j, 0)),
        ],
        all_of((rows, D)),
        kept((rows, D))[0],
        [pltpu.VMEM((rows, D), f32)],
        4 << 30,
        (stored(nf), w_up, w_down),
        None,
        "own_hidden",
    )
    up_far, down_far = after(up_far, own), after(down_far, own)
    ups += [up_far, *up_partners, *partners([up_far])]
    downs += [down_far, *down_partners, *partners([down_far])]
    memory_other, hid = lax.optimization_barrier((memory_other, hid))
    out_own, out_other = call(
        other_hidden_kernel,
        (1,),
        [all_of((rows, D))] * 3 + [ANY] * 16,
        [all_of((U, F, HALF))] * 2,
        arrays((U, F, HALF), (U, F, HALF)),
        [
            pltpu.VMEM((4, D, HALF), bf16),
            pltpu.VMEM((2048, D), bf16),
            pltpu.VMEM((rows, D), f32),
            pltpu.SemaphoreType.DMA((5,)),
        ],
        4 << 30,
        (stored(nf), stored(hid), stored(own), *ups, *downs),
        scalars,
        "other_hidden",
    )
    memory_out = joined(cut(memory, h * HALF, HALF, 2), memory_other, h, 0)
    encoded = joined(out_own, moved(out_other, "m"), h, 0)
    return encoded, memory_out


def solution(mesh):
    in_specs = (
        P(None, "tm", None),
        P(),
        P(None, "tm"),
        P(None, "tm", "mp"),
        P(None, "mp"),
        P(),
        P(None, "mp"),
        P(None, "mp"),
        P(None, "mp"),
        P("mp", None),
        P(),
        P(None, "mp"),
        P("mp", None),
    )
    out_specs = (P(None, "tm", "mp"), P(None, "tm", "mp"))

    return jax.shard_map(body, mesh=mesh, in_specs=in_specs, out_specs=out_specs, check_vma=False)
```

```python
import jax
import jax.numpy as jnp
from jax import lax
from jax.experimental import pallas as pl
from jax.experimental.pallas import tpu as pltpu
from jax.sharding import PartitionSpec as P


D = 1024
HALF = 512
SEG = 4
LC = 32
RC = 4
M = 32
NX, NZ, NY, NC = 4, 4, 4, 2
TM = NX * NZ * NY * NC
U = 2
F = 256
S = 64
EXT = 320
QB, KB = 160, 256
KF = 192
epsilon = 1e-05
bf16, f32, i32 = jnp.bfloat16, jnp.float32, jnp.int32
AXES = ("tm", "mp")
GRANTS = {
    "pack": 48,
    "front": 48,
    "own_heads": 48,
    "other_heads": 48,
    "own_hidden": 48,
    "other_hidden": 48,
}


def place(x, z, y, c, m):
    return ((((x % NX) * NZ + z) * NY + y % NY) * NC + c % NC) * 2 + m % 2


def route(step):
    dx, dy, dc, dm = step
    return [
        (place(x, z, y, c, m), place(x + dx, z, y + dy, c + dc, m + dm))
        for x in range(NX)
        for z in range(NZ)
        for y in range(NY)
        for c in range(NC)
        for m in range(2)
    ]


STEPS = {
    ("x", 1): (1, 0, 0, 0),
    ("x", -1): (-1, 0, 0, 0),
    ("y", 1): (0, 1, 0, 0),
    ("y", -1): (0, -1, 0, 0),
    ("c", 1): (0, 0, 1, 0),
    ("m", 1): (0, 0, 0, 1),
}


def moved(array, axis, by=1):
    return lax.ppermute(array, AXES, route(STEPS[axis, by]))


def along_frames(array, by):
    pairs = [
        (t * 2 + m, (t + by) * 2 + m) for t in range(TM) for m in range(2) if 0 <= t + by < TM
    ]
    return lax.ppermute(array, AXES, pairs)


def after(value, *earlier):
    return lax.optimization_barrier((value, *earlier))[0]


def both_ways(array, axis, way):
    back = moved(array, axis, way)
    front = moved(array, axis, -way)
    return back, front


def partners(blocks):
    return [moved(b, "c") for b in blocks]


def each_piece(first, way, where, halves, act):
    x, y, c = where
    far = [(0, 0, 4), (way, 0, 4), (-way, 0, 4)]
    far += [(2, 0, 2), (2, 2, 4)] if halves else [(2, 0, 4)]
    for i, (a2, low, high) in enumerate(far):

        def step(j, carry):
            a1 = jnp.where(j == 0, 0, jnp.where(j == 1, -way, jnp.where(j == 2, way, 2)))
            px = (x + (a1 if first == "x" else a2)) & 3
            py = (y + (a2 if first == "x" else a1)) & 3
            for k in range(2):
                pc = c if k == 0 else 1 - c
                act(i + len(far) * k, j - low, px * 8 + py * 2 + pc)
            return carry

        lax.fori_loop(low, high, step, 0)


def dot(a, b):
    return jnp.dot(a, b, preferred_element_type=f32)


def normed(values, gain):
    center = jnp.sum(values, axis=-1, keepdims=True) * (1.0 / D)
    shifted = values - center
    spread_ = jnp.sum(shifted * shifted, axis=-1, keepdims=True) * (1.0 / D)
    return shifted * lax.rsqrt(spread_ + epsilon) * gain


def gelu(v):
    inner = 0.7978845608028654 * (v + 0.044715 * (v * v * v))
    return 0.5 * v * (1.0 + jnp.tanh(inner))


def pack_kernel(sc, wq, wk, wv, wo, wu, wd, mem, s1, up, down):
    s1[:, :HALF] = wq[...]
    s1[:, HALF : 2 * HALF] = wk[...]
    s1[:, 2 * HALF : 3 * HALF] = wv[...]
    s1[:16, 3 * HALF :] = wo[:, :HALF]
    s1[16:, 3 * HALF :] = wo[:, HALF:]
    up[:, :2048] = wu[...]
    down[...] = wd[...]
    for i in range(4):
        at = slice(2048 + HALF * i, 2048 + HALF * i + HALF)
        up[:, at] = mem[i // 2, 32 * (i % 2) : 32 * (i % 2) + 32, :]


def front_kernel(
    sc, fb, left, right, wf_own, wf_a, wf_b, gain, wq, wk, wv, x_out, n_out, q, k, v, xs, fbs
):
    u = pl.program_id(0)
    h, c = sc[2], sc[5]
    fbs[:LC] = left[0]
    fbs[LC : LC + F] = fb[0]
    fbs[LC + F : LC + F + 16] = right[0]
    fbs[LC + F + 16 :] = jnp.zeros((16, 320), bf16)
    rows = fbs[...]
    pos = sc[3] * F - LC + lax.broadcasted_iota(i32, (EXT, 1), 0)
    valid = pos < sc[u]

    def put(at, width, w):
        part = jnp.where(valid, dot(rows, w[...]), 0.0).astype(bf16)
        xs[:, pl.ds(pl.multiple_of(at, 256), width)] = part

    other = (1 - h) * HALF
    put(h * HALF, HALF, wf_own)
    put(other + c * 256, 256, wf_a)
    put(other + (1 - c) * 256, 256, wf_b)
    x_out[0] = xs[LC : LC + F, :]
    g = gain[...]
    n_out[0, :EXT, :] = normed(xs[...].astype(f32), g).astype(bf16)
    seg = lax.broadcasted_iota(i32, (S, F), 0)
    frame = lax.broadcasted_iota(i32, (S, F), 1)
    pool = jnp.where(frame // SEG == seg, 0.25, 0.0).astype(bf16)
    n_out[0, EXT:, :] = normed(dot(pool, xs[LC : LC + F, :]), g).astype(bf16)
    project(n_out, wq, wk, wv, q, k, v)


def project(n, wq, wk, wv, q, k, v):
    q[0, :F, :] = (dot(n[0, LC : LC + F, :], wq[...]) * 0.125).astype(bf16)
    q[0, F:, :] = (dot(n[0, EXT:, :], wq[...]) * 0.125).astype(bf16)
    k[0] = dot(n[0, :EXT, :], wk[...]).astype(bf16)
    v[0] = dot(n[0, :EXT, :], wv[...]).astype(bf16)


def mask_of(sc, u, b, begins):
    t = sc[3]
    shape = (QB, S)
    r = lax.broadcasted_iota(i32, shape, 0)
    col = lax.broadcasted_iota(i32, shape, 1)
    local = 32 * b + jnp.where(r < 128, r // SEG, r - 128)
    begin = begins[pl.ds(2 * sc[2] + u, 1), :]
    floor = jnp.sum(jnp.where(col == local, begin, 0), axis=-1, keepdims=True)
    r = lax.broadcasted_iota(i32, (QB, 1), 0)
    seg = t * S + 32 * b + jnp.where(r < 128, r // SEG, r - 128)
    k = lax.broadcasted_iota(i32, (QB, KB), 1)
    pos = t * F - LC + 128 * b + k
    bank = t * S - M + 32 * b + k - KF
    low = jnp.maximum(seg * SEG - LC, 0)
    high = jnp.minimum((seg + 1) * SEG + RC, sc[u])
    sees_frame = (k < KF) & (pos >= low) & (pos < high)
    sees_bank = (k >= KF) & (bank >= floor) & (bank <= seg - 1)
    return jnp.where(sees_frame | sees_bank, 0.0, -1e30).astype(f32)


def attend(sc, u, begins, q, k, v, mk, mv, ctx):
    low = lax.broadcasted_iota(i32, (1, 128), 1) < 64

    def block(b, carry):
        mask = mask_of(sc, u, b, begins)
        masks = jnp.concatenate([mask, mask], axis=0)
        at = pl.multiple_of(b * 128, 128)
        few = pl.multiple_of(b * 32, 32)
        fr, sm = pl.ds(at, 128), pl.ds(F + few, 32)
        kr, mr = pl.ds(at, KF), pl.ds(few, 64)
        for p in range(4):
            lanes = slice(128 * p, 128 * p + 128)
            qb = jnp.concatenate([q[0, fr, lanes], q[0, sm, lanes]], axis=0)
            zero = jnp.zeros_like(qb)
            pair = jnp.concatenate([jnp.where(low, qb, zero), jnp.where(low, zero, qb)], axis=0)
            keys = jnp.concatenate([k[0, kr, lanes], mk[mr, lanes]], axis=0)
            values = jnp.concatenate([v[0, kr, lanes], mv[mr, lanes]], axis=0)
            scores = lax.dot_general(
                pair, keys, (((1,), (1,)), ((), ())), preferred_element_type=f32
            )
            weights = jnp.exp(scores + masks)
            total = jnp.sum(weights, axis=-1, keepdims=True)
            shares = (weights * (1.0 / total)).astype(bf16)
            mixed = dot(shares, values)
            part = jnp.where(low, mixed[:QB], mixed[QB:]).astype(bf16)
            ctx[0, fr, lanes] = part[:128]
            ctx[0, sm, lanes] = part[128:]
        return carry

    lax.fori_loop(0, 2, block, 0)


def own_heads_kernel(
    sc, mem_a, mem_b, halo_a, halo_b, begins, gain, wk, wv, q, k, v, ctx, nm, mk, mv, ms
):
    h = sc[2]
    mine = pl.ds(pl.multiple_of(h * HALF, HALF), HALF)
    theirs = pl.ds(pl.multiple_of((1 - h) * HALF, HALF), HALF)
    ms[:M, mine] = halo_a[0]
    ms[M:, mine] = mem_a[0]
    ms[:M, theirs] = halo_b[0]
    ms[M : M + 32, theirs] = mem_b[:, :HALF]
    ms[M + 32 :, theirs] = mem_b[:, HALF:]
    nm[0] = normed(ms[...].astype(f32), gain[...]).astype(bf16)
    mk[...] = dot(nm[0], wk[...]).astype(bf16)
    mv[...] = dot(nm[0], wv[...]).astype(bf16)
    attend(sc, pl.program_id(0), begins, q, k, v, mk, mv, ctx)


def other_heads_kernel(*refs):
    sc, n, nm, begins, ctx_own, x, wo_own, gain = refs[:8]
    parts = refs[8:18]
    hid, nf, memory = refs[18:21]
    wqkv, wo, q, k, v, mk, mv, ctx, sem = refs[21:]
    u = pl.program_id(0)
    where = (sc[4], sc[6], sc[5])

    @pl.when(u == 0)
    def _():
        def fetch(r, j, at):
            rows = pl.ds(pl.multiple_of(at * 32, 32), 32)
            src = parts[r].at[j, :, : 3 * HALF]
            pltpu.make_async_copy(src, wqkv.at[rows], sem.at[0]).start()

        def fetch_out(r, j, at):
            few = pl.ds(pl.multiple_of(at * 16, 16), 16)
            for s in range(2):
                src = parts[r].at[j, 16 * s : 16 * s + 16, 3 * HALF :]
                dst = wo.at[few, HALF * s : HALF * s + HALF]
                pltpu.make_async_copy(src, dst, sem.at[1]).start()

        each_piece("y", -1, where, True, fetch)
        each_piece("y", -1, where, True, fetch_out)

    mine = dot(ctx_own[0], wo_own[...]).astype(bf16).astype(f32)

    @pl.when(u == 0)
    def _():
        pltpu.make_async_copy(wqkv, wqkv, sem.at[0]).wait()

    wk, wv = wqkv.at[:, HALF : 2 * HALF], wqkv.at[:, 2 * HALF :]
    project(n, wqkv.at[:, :HALF], wk, wv, q, k, v)
    mk[...] = dot(nm[0], wk[...]).astype(bf16)
    mv[...] = dot(nm[0], wv[...]).astype(bf16)
    attend(sc, u, begins, q, k, v, mk, mv, ctx)

    @pl.when(u == 0)
    def _():
        pltpu.make_async_copy(wo, wo, sem.at[1]).wait()

    theirs = dot(ctx[0], wo[...]).astype(bf16).astype(f32)
    both = mine + theirs
    seg = sc[3] * S + lax.broadcasted_iota(i32, (S, 1), 0)
    memory[0] = jnp.where(seg * SEG < sc[u], both[F:], 0.0).astype(bf16)
    residual = (x[0].astype(f32) + both[:F]).astype(bf16)
    hid[...] = residual
    nf[...] = normed(residual.astype(f32), gain[...]).astype(bf16)


def own_hidden_kernel(nf, wu, wd, out, acc):
    j = pl.program_id(0)

    def some(r, carry):
        rows = pl.ds(pl.multiple_of(r * F, F), F)
        hidden = gelu(dot(nf[rows], wu[...])).astype(bf16)
        part = dot(hidden, wd[...])
        acc[rows] = jnp.where(j == 0, part, acc[rows] + part)
        return carry

    lax.fori_loop(0, U, some, 0)

    @pl.when(j == pl.num_programs(0) - 1)
    def _():
        out[...] = acc[...].astype(bf16)


def other_hidden_kernel(*refs):
    sc, nf, hid, own = refs[:4]
    ups, downs = refs[4:12], refs[12:20]
    out_own, out_other = refs[20:22]
    wu, wd, acc, sem = refs[22:]
    where = (sc[4], sc[6], sc[5])

    x = sc[4]

    def fetch_up(i, carry):
        ahead = jnp.where(i == 0, 0, jnp.where(i == 1, -1, jnp.where(i == 2, 1, 2)))
        chunk = (x + ahead) & 3
        cols = pl.ds(pl.multiple_of(chunk * HALF, HALF), HALF)

        def fetch(r, j, at):
            rows = pl.ds(pl.multiple_of(at * 32, 32), 32)
            pltpu.make_async_copy(ups[r].at[j, :, cols], wu.at[i, rows], sem.at[i]).start()

        each_piece("x", 1, where, False, fetch)
        return carry

    def fetch_down(r, j, at):
        rows = pl.ds(pl.multiple_of((at & 7) * 64, 64), 64)
        slot = r % 4
        copy = pltpu.make_async_copy(downs[r].at[j], wd.at[slot, rows], sem.at[4 + slot])
        copy.start()

    fetch_up(0, 0)
    each_piece("y", -1, where, False, fetch_down)
    lax.fori_loop(1, 4, fetch_up, 0)
    acc[...] = jnp.zeros_like(acc)

    def step(i, carry):
        pltpu.make_async_copy(wu.at[i], wu.at[i], sem.at[i]).wait()
        pltpu.make_async_copy(wd.at[i], wd.at[i], sem.at[4 + i]).wait()

        def some(r, carry):
            rows = pl.ds(pl.multiple_of(r * F, F), F)
            hidden = gelu(dot(nf[rows], wu[i])).astype(bf16)
            acc[rows] += dot(hidden, wd[i])
            return carry

        return lax.fori_loop(0, U, some, carry)

    lax.fori_loop(0, 4, step, 0)
    h = sc[2]
    row = lax.broadcasted_iota(i32, (F, 1), 0)
    for u in range(U):
        valid = sc[3] * F + row < sc[u]
        at = slice(F * u, F * u + F)
        for out, start in ((out_own, h * HALF), (out_other, (1 - h) * HALF)):
            cols = pl.ds(pl.multiple_of(start, HALF), HALF)
            feed = own[at, cols].astype(f32) + acc[at, cols].astype(bf16).astype(f32)
            whole = hid[at, cols].astype(f32) + feed
            out[u] = jnp.where(valid, whole, 0.0).astype(bf16)


def one(shape):
    return pl.BlockSpec((1,) + shape, lambda u, *_: (u,) + (0,) * len(shape))


def all_of(shape):
    return pl.BlockSpec(shape, lambda *_: (0,) * len(shape))


ANY = pl.BlockSpec(memory_space=pl.ANY)


def arrays(*shapes):
    return [jax.ShapeDtypeStruct(s, bf16) for s in shapes]


def kept(*shapes):
    return [pltpu.HBM(s, bf16) for s in shapes]


def stored(array):
    return pltpu.with_memory_space_constraint(array, pltpu.HBM)


def call(kernel, grid, ins, outs, out_shape, scratch, flops, args, scalars=None, name=None):
    spec = pltpu.PrefetchScalarGridSpec(
        num_scalar_prefetch=0 if scalars is None else 1,
        grid=grid,
        in_specs=ins,
        out_specs=outs,
        scratch_shapes=scratch,
    )
    given = list(args) if scalars is None else [scalars, *args]
    return pl.pallas_call(
        kernel,
        grid_spec=spec,
        out_shape=out_shape,
        compiler_params=pltpu.CompilerParams(
            dimension_semantics=("arbitrary",) * len(grid), vmem_limit_bytes=GRANTS[name] << 20
        ),
        cost_estimate=pl.CostEstimate(
            flops=flops, bytes_accessed=8 << 20, transcendentals=1 << 20
        ),
    )(*given)


def cut(array, at, size, dim):
    return lax.dynamic_slice_in_dim(array, at, size, dim)


def joined(own, other, h, dim):
    return jnp.where(
        h == 0,
        jnp.concatenate([own, other], axis=dim),
        jnp.concatenate([other, own], axis=dim),
    )


def body(
    filterbank,
    lengths,
    bank_begin,
    memory_in,
    w_front,
    gain_attn,
    w_query,
    w_key,
    w_value,
    w_out,
    gain_ffn,
    w_up,
    w_down,
):
    t, h = lax.axis_index("tm"), lax.axis_index("mp")
    x_at, y_at, c_at = t // (NZ * NY * NC), (t // NC) % NY, t % NC
    piece = x_at * 8 + y_at * 2 + c_at
    lens = cut(lengths, 2 * h, 2, 0)
    scalars = jnp.concatenate([lens, jnp.stack([h, t, x_at, c_at, y_at, piece]).astype(i32)])

    gain_a, gain_f = gain_attn.reshape(1, D), gain_ffn.reshape(1, D)

    wf_cut = cut(w_front, c_at * 256, 256, 1)
    wf_a = moved(wf_cut, "m")
    wf_b = moved(wf_a, "c")

    def piece_of(rows, width):
        return pl.BlockSpec((rows, width), lambda i, sc: (sc[7], 0))

    weights = [stored(w) for w in (w_query, w_key, w_value, w_out, w_up, w_down)]
    w_query, w_key, w_value, w_out, w_up, w_down = weights
    memory_all = stored(memory_in)
    s1, up, down = call(
        pack_kernel,
        (1,),
        [piece_of(32, HALF)] * 3 + [piece_of(16, D), piece_of(32, 2048), piece_of(64, D)]
        + [pl.BlockSpec((2, S, HALF), lambda i, sc: (1 - sc[2], 0, 0))],
        [all_of((32, 2048)), all_of((32, 4096)), all_of((64, D))],
        arrays((32, 2048), (32, 4096), (64, D)),
        [],
        1 << 20,
        (w_query, w_key, w_value, w_out, w_up, w_down, memory_all),
        after(scalars, wf_cut),
        "pack",
    )
    filterbank = after(filterbank, up)
    s1 = moved(s1, "m")
    up = moved(up, "m")
    down = moved(down, "m")
    back, front = both_ways(s1, "y", -1)
    third = moved(back, "y", -1)
    filled1 = jnp.stack([s1, back, front, third])
    back1, front1 = both_ways(filled1, "x", 1)

    fb = filterbank.reshape(4, F, 320)
    mine = cut(fb, 2 * h, 2, 0)
    left = along_frames(mine[:, F - LC :], 1)
    right = along_frames(mine[:, :16], -1)
    halo_own = along_frames(cut(memory_in, 2 * h, 2, 0)[:, S - M :], 1)

    x, n, q, kk, v = call(
        front_kernel,
        (U,),
        [pl.BlockSpec((1, F, 320), lambda u, sc: (2 * sc[2] + u, 0, 0))]
        + [one((LC, 320)), one((16, 320))]
        + [all_of((320, HALF)), all_of((320, 256)), all_of((320, 256))]
        + [all_of((1, D))]
        + [all_of((D, HALF))] * 3,
        [one((F, D)), one((EXT + S, D))] + [one((EXT, HALF))] * 3,
        kept((U, F, D), (U, EXT + S, D), *[(U, EXT, HALF)] * 3),
        [pltpu.VMEM((EXT, D), bf16), pltpu.VMEM((EXT, 320), bf16)],
        2 * 640 * 1024 * 1536,
        (fb, left, right, w_front, wf_a, wf_b, gain_a, w_query, w_key, w_value),
        scalars,
        "front",
    )
    mem_other, up = up, up[:, :2048]
    late = [mem_other[:, at : at + HALF] for at in (2560, 3584)]
    halo_other = along_frames(jnp.stack(late), 1)
    up_back, up_front = both_ways(up, "x", 1)
    down_back, down_front = both_ways(down, "y", -1)
    ctx, nm = call(
        own_heads_kernel,
        (U,),
        [pl.BlockSpec((1, S, HALF), lambda u, sc: (2 * sc[2] + u, 0, 0))]
        + [pl.BlockSpec((32, D), lambda u, sc: (0, 2 + u))]
        + [one((M, HALF))] * 2
        + [all_of((4, S)), all_of((1, D)), all_of((D, HALF)), all_of((D, HALF))]
        + [one((EXT, HALF))] * 3,
        [one((EXT, HALF)), one((S + M, D))],
        kept((U, EXT, HALF), (U, S + M, D)),
        [pltpu.VMEM((S + M, HALF), bf16)] * 2 + [pltpu.VMEM((S + M, D), bf16)],
        2 << 30,
        (memory_all, mem_other, halo_own, halo_other, bank_begin, gain_a, w_key, w_value, *map(stored, (q, kk, v))),
        scalars,
        "own_heads",
    )
    up_back, down_back = after(up_back, ctx), after(down_back, ctx)
    ups = jnp.stack([up, up_back, up_front, moved(up_back, "x", 1)])
    downs = jnp.stack([down, down_back, down_front, moved(down_back, "y", -1)])
    ups = [ups, *both_ways(ups, "y", -1)]
    downs = [downs, *both_ways(downs, "x", 1)]
    back1, front1, filled1 = after(back1, ctx), after(front1, ctx), after(filled1, ctx)
    blocks1 = [filled1, back1, front1]
    blocks1 += [moved(back1[:2], "x", 1), moved(front1[2:], "x", -1)]
    blocks1 += partners(blocks1)
    hid, nf, memory = call(
        other_heads_kernel,
        (U,),
        [one((EXT + S, D)), one((S + M, D)), all_of((4, S)), one((EXT, HALF)), one((F, D))]
        + [all_of((HALF, D)), all_of((1, D))]
        + [ANY] * 10,
        [pl.BlockSpec((F, D), lambda u, *_: (u, 0))] * 2 + [one((S, D))],
        kept((U * F, D), (U * F, D)) + arrays((U, S, D)),
        [pltpu.VMEM((D, 3 * HALF), bf16), pltpu.VMEM((HALF, D), bf16)]
        + [pltpu.VMEM((1, EXT, HALF), bf16)] * 3
        + [pltpu.VMEM((S + M, HALF), bf16)] * 2
        + [pltpu.VMEM((1, EXT, HALF), bf16), pltpu.SemaphoreType.DMA((2,))],
        6 << 30,
        (stored(n), stored(nm), bank_begin, stored(ctx), stored(x), w_out, gain_f, *blocks1),
        scalars,
        "other_heads",
    )
    ups = [after(w, hid) for w in ups]
    downs = [after(w, hid) for w in downs]
    up_far = moved(ups[1], "y", -1)
    down_far = moved(downs[1], "x", 1)
    up_partners, down_partners = partners(ups), partners(downs)
    memory_other = moved(cut(memory, (1 - h) * HALF, HALF, 2), "m")
    rows = U * F
    own = call(
        own_hidden_kernel,
        (4,),
        [
            all_of((rows, D)),
            pl.BlockSpec((D, HALF), lambda j: (0, j)),
            pl.BlockSpec((HALF, D), lambda j: (j, 0)),
        ],
        all_of((rows, D)),
        kept((rows, D))[0],
        [pltpu.VMEM((rows, D), f32)],
        4 << 30,
        (stored(nf), w_up, w_down),
        None,
        "own_hidden",
    )
    up_far, down_far = after(up_far, own), after(down_far, own)
    ups += [up_far, *up_partners, *partners([up_far])]
    downs += [down_far, *down_partners, *partners([down_far])]
    memory_other, hid = lax.optimization_barrier((memory_other, hid))
    out_own, out_other = call(
        other_hidden_kernel,
        (1,),
        [all_of((rows, D))] * 3 + [ANY] * 16,
        [all_of((U, F, HALF))] * 2,
        arrays((U, F, HALF), (U, F, HALF)),
        [
            pltpu.VMEM((4, D, HALF), bf16),
            pltpu.VMEM((4, HALF, D), bf16),
            pltpu.VMEM((rows, D), f32),
            pltpu.SemaphoreType.DMA((8,)),
        ],
        4 << 30,
        (stored(nf), stored(hid), stored(own), *ups, *downs),
        scalars,
        "other_hidden",
    )
    memory_out = joined(cut(memory, h * HALF, HALF, 2), memory_other, h, 0)
    encoded = joined(out_own, moved(out_other, "m"), h, 0)
    return encoded, memory_out


def solution(mesh):
    in_specs = (
        P(None, "tm", None),
        P(),
        P(None, "tm"),
        P(None, "tm", "mp"),
        P(None, "mp"),
        P(),
        P(None, "mp"),
        P(None, "mp"),
        P(None, "mp"),
        P("mp", None),
        P(),
        P(None, "mp"),
        P("mp", None),
    )
    out_specs = (P(None, "tm", "mp"), P(None, "tm", "mp"))

    return jax.shard_map(body, mesh=mesh, in_specs=in_specs, out_specs=out_specs, check_vma=False)
```
